32 devices in a mesh: section: 2 (over x), dp: 16 (over z, y, core).
Axes of the slice: x: 2, y: 2, z: 4, core: 2. Of those that a mesh axis runs over, the one named last changes fastest.
Arguments:
- section_inputs: bfloat16 [2, 2048, 8192], P('section', 'dp'), may hold values from -6 to 6
- teacher_states: bfloat16 [2048, 8192], P('dp'), may hold values from -6 to 6
- confidence: int32 [2048], P('dp'), may hold values from 1 to 256
- gains: float32 [2, 8192], P('section'), may hold values from 0.1 to 1.9
- w_down: bfloat16 [2, 8192, 256], P('section', 'dp'), may hold values from -0.0625 to 0.0625
- w_up: bfloat16 [2, 8192, 256], P('section', 'dp'), may hold values from -0.375 to 0.375
Outputs:
- input_grads: bfloat16 [2, 2048, 8192], P('section', 'dp')
- grad_down: float32 [2, 8192, 256], P('section', 'dp')
- grad_up: float32 [2, 8192, 256], P('section', 'dp')
- grad_gain: float32 [2, 8192], P('section', 'dp')
The draws below stay inside these ranges and needn't reach their ends.
All inputs are finite; a program needn't handle non-finite values.
Results may differ from the reference program's by a relative error of at most 0.013.
Values may be sent and summed in bfloat16 or wider, within the bound.
No kernel may reach another device: no remote copies, remote signals or barrier semaphores. Data moves between devices by JAX's collectives and lax.ppermute only.
A program may use at most 64 MiB of HBM per device.

```python
import jax
import jax.numpy as jnp
from jax import lax

D = 8192
RANK = 256
TOK_DEV = 128
TOKENS = 2048
SECTIONS = 2


def with_ends(entries, stream_key, smallest, top_value):
    longest = entries.shape.index(max(entries.shape))
    spots = []
    for shift in (0, 1):
        where = [jax.random.randint(jax.random.fold_in(stream_key, axis), (), 0, length) for axis, length in enumerate(entries.shape)]
        where[longest] = (where[longest] + shift) % entries.shape[longest]
        spots.append(tuple(where))
    return entries.at[spots[0]].set(smallest).at[spots[1]].set(top_value)


def spiked(values, key, source, target, parts, factor):
    owner, partner = [(jnp.arange(values.shape[position]) // (values.shape[position] // parts)).reshape([-1 if axis == position else 1 for axis in range(values.ndim)]) for position in (source, target)]
    chosen = jax.random.permutation(key, parts)[partner]
    strong = (owner == chosen) | (owner == (partner + parts // 2) % parts)
    return jnp.where(strong, factor * values, values)


def block_scale(key, shape, shards, least, largest):
    factor_of, own = 1.0, jax.random.fold_in(key, 6)
    for axis_at, parts in shards:
        heights = jnp.exp(jax.random.uniform(jax.random.fold_in(own, axis_at), (parts,), jnp.float32, least / len(shards), largest / len(shards)))
        factor_of = factor_of * jnp.repeat(heights, shape[axis_at] // parts).reshape([-1 if axis == axis_at else 1 for axis in range(len(shape))])
    return factor_of


def centred(rng, dims, spread, most, shards=(), kind=jnp.bfloat16):
    drawn = spread * jax.random.normal(rng, dims, jnp.float32)
    if shards:
        drawn = drawn * block_scale(rng, dims, shards, -0.22, 0.18)
    return jnp.clip(drawn, -most, most).astype(kind)


def bell_draw_with(own_key, extent, scale, bound, cuts, heavy, dtype=jnp.bfloat16):
    entries = scale * jax.random.normal(own_key, extent, jnp.float32)
    if cuts:
        entries = entries * block_scale(own_key, extent, cuts, -0.22, 0.18)
    return jnp.clip(spiked(entries, jax.random.fold_in(own_key, 3), *heavy), -bound, bound).astype(dtype)


def setup_inputs(seed: int = 0) -> dict:
    key_of = jax.random.split(jax.random.key(seed), 7)
    return {
        "section_inputs": bell_draw_with(key_of[0], (SECTIONS, TOKENS, D), 1.0, 6.0, ((0, 2), (1, 16)), (1, 2, 16, 2.0)),
        "teacher_states": centred(key_of[1], (TOKENS, D), 1.0, 6.0, ((0, 16),)),
        "confidence": with_ends(jax.random.randint(key_of[2], (TOKENS,), 1, 257), jax.random.fold_in(key_of[2], 1), 1, 256).astype(jnp.int32),
        "gains": jnp.clip(1.0 + 0.18 * jax.random.normal(key_of[3], (SECTIONS, D), jnp.float32), 0.1, 1.9),
        "w_down": centred(key_of[4], (SECTIONS, D, RANK), D ** -0.5, 0.0625, ((0, 2), (1, 16))),
        "w_up": centred(key_of[5], (SECTIONS, D, RANK), RANK ** -0.5, 0.375, ((0, 2), (1, 16))),
    }


EPSILON = 1e-05

def forward_part(inputs, gain, w_down):
    values = inputs.astype(jnp.float32)
    inverse = lax.rsqrt(lax.optimization_barrier(jnp.mean(values * values, axis=-1, keepdims=True)) + EPSILON)
    normed = values * inverse
    scaled = (normed * gain).astype(jnp.bfloat16)
    preact = jnp.dot(scaled, w_down, preferred_element_type=jnp.float32)
    hidden = jax.nn.silu(preact).astype(jnp.bfloat16)
    return (values, inverse, normed, scaled, preact, hidden)

def reference(section_inputs, teacher_states, confidence, gains, w_down, w_up):
    weight_rows = confidence.astype(jnp.float32) / 256.0
    cotangent = None
    grads_in = []
    downs = []
    uppers = []
    gain_list = []
    for layer in range(SECTIONS - 1, -1, -1):
        gain = gains[layer]
        values, inverse, normed, scaled, preact, hidden = forward_part(section_inputs[layer], gain, w_down[layer])
        if cotangent is None:
            branch = jnp.dot(hidden, w_up[layer].T, preferred_element_type=jnp.float32)
            output = values + branch
            cotangent = (weight_rows[:, None] * (output - teacher_states.astype(jnp.float32))).astype(jnp.bfloat16)
        hidden_grad = jnp.dot(cotangent, w_up[layer], preferred_element_type=jnp.float32)
        sigmoid_val = jax.nn.sigmoid(preact)
        pre_grad = (hidden_grad * sigmoid_val * (1.0 + preact * (1.0 - sigmoid_val))).astype(jnp.bfloat16)
        normed_grad = jnp.dot(pre_grad, w_down[layer].T, preferred_element_type=jnp.float32)
        grad_down = jnp.dot(scaled.T, pre_grad, preferred_element_type=jnp.float32) / TOK_DEV
        grad_up = jnp.dot(cotangent.T, hidden, preferred_element_type=jnp.float32) / TOK_DEV
        grad_gain = lax.optimization_barrier(jnp.sum(normed_grad * normed, axis=0)) / TOK_DEV
        scaled_grad = normed_grad * gain
        input_grad = cotangent.astype(jnp.float32) + inverse * (scaled_grad - normed * lax.optimization_barrier(jnp.mean(scaled_grad * normed, axis=-1, keepdims=True)))
        input_grad = input_grad.astype(jnp.bfloat16)
        grads_in.append(input_grad)
        downs.append(grad_down)
        uppers.append(grad_up)
        gain_list.append(grad_gain)
        cotangent = input_grad
    grads_in = grads_in[::-1]
    downs = downs[::-1]
    uppers = uppers[::-1]
    gain_list = gain_list[::-1]
    return (jnp.stack(grads_in), jnp.stack(downs), jnp.stack(uppers), jnp.stack(gain_list))
```

```python
import jax
import jax.numpy as jnp
import numpy as np
from jax import lax
from jax.experimental import pallas as pl
from jax.experimental.pallas import tpu as pltpu
from jax.sharding import PartitionSpec as P

Z_CHIPS = 4
CORES = 2
EPSILON = 1e-05
F32 = jnp.float32
BF16 = jnp.bfloat16


def ring_of_chips(chips):
    rows = chips // Z_CHIPS
    cycle = []
    for z in range(Z_CHIPS):
        ys = range(1, rows) if z % 2 == 0 else range(rows - 1, 0, -1)
        cycle += [z * rows + y for y in ys]
    return cycle + [z * rows for z in range(Z_CHIPS - 1, -1, -1)]


class Routes:
    def __init__(self, devices):
        self.ring = ring_of_chips(devices // CORES)
        n = self.n = len(self.ring)
        self.half = n // 2
        self.partner = [(i, i ^ 1) for i in range(devices)]
        self.onward_by_core = [
            [(self.ring[i] * CORES + c, self.ring[(i + 1 - 2 * c) % n] * CORES + c) for i in range(n)]
            for c in range(CORES)
        ]
        self.onward = self.onward_by_core[0] + self.onward_by_core[1]
        table = np.zeros((devices, n), np.int32)
        for i, chip in enumerate(self.ring):
            for c in range(CORES):
                sign = 1 - 2 * c
                steps = [0] + [-k for k in range(1, self.half)] + list(range(1, self.half)) + [self.half]
                table[chip * CORES + c] = [self.ring[(i + sign * s) % n] for s in steps]
        self.table = table

    def behind(self, k):
        return k

    def ahead(self, k):
        return self.half - 1 + k

    @property
    def opposite(self):
        return self.n - 1


def arrange_kernel(ids, x_ref, t_ref, gain_ref, inv_ref, x_out, t_out, scaled_out, gain_out):
    x = x_ref[...]
    x_out[0] = x
    t_out[0] = t_ref[...]
    gain = gain_ref[...]
    gain_out[0] = gain
    scaled_out[0] = ((x.astype(F32) * inv_ref[...]) * gain).astype(BF16)


def arrange(ids, x, teacher, gain, inverse):
    tokens, width = x.shape
    n = ids.shape[0]
    block = width // n
    return pl.pallas_call(
        arrange_kernel,
        grid_spec=pltpu.PrefetchScalarGridSpec(
            num_scalar_prefetch=1,
            grid=(n,),
            in_specs=[
                pl.BlockSpec((tokens, block), lambda j, ids: (0, ids[j])),
                pl.BlockSpec((tokens, block), lambda j, ids: (0, ids[j])),
                pl.BlockSpec((1, block), lambda j, ids: (0, ids[j])),
                pl.BlockSpec((tokens, 1), lambda j, ids: (0, 0)),
            ],
            out_specs=[
                pl.BlockSpec((1, tokens, block), lambda j, ids: (j, 0, 0)),
                pl.BlockSpec((1, tokens, block), lambda j, ids: (j, 0, 0)),
                pl.BlockSpec((1, tokens, block), lambda j, ids: (j, 0, 0)),
                pl.BlockSpec((1, 1, block), lambda j, ids: (j, 0, 0)),
            ],
        ),
        out_shape=[
            jax.ShapeDtypeStruct((n, tokens, block), BF16),
            jax.ShapeDtypeStruct((n, tokens, block), BF16),
            jax.ShapeDtypeStruct((n, tokens, block), BF16),
            jax.ShapeDtypeStruct((n, 1, block), F32),
        ],
        cost_estimate=pl.CostEstimate(flops=4 * tokens * width, bytes_accessed=10 * tokens * width, transcendentals=0),
        name="arrange",
    )(ids, x, teacher, gain, inverse)


def finish_kernel(ids, cot_ref, x_ref, down_ref, gain_ref, pre_ref, inv_ref, mean_ref, out_ref):
    grad = lax.dot_general(pre_ref[...], down_ref[0], (((1,), (1,)), ((), ())), preferred_element_type=F32)
    normed = x_ref[0].astype(F32) * inv_ref[...]
    out = cot_ref[0].astype(F32) + inv_ref[...] * (grad * gain_ref[0] - normed * mean_ref[...])
    out_ref[...] = out.astype(BF16)


def finish(ids, cot, x, down, gain, pre_grad, inverse, mean):
    n, tokens, block = cot.shape
    rank = pre_grad.shape[1]
    return pl.pallas_call(
        finish_kernel,
        grid_spec=pltpu.PrefetchScalarGridSpec(
            num_scalar_prefetch=1,
            grid=(n,),
            in_specs=[
                pl.BlockSpec((1, tokens, block), lambda j, ids: (j, 0, 0)),
                pl.BlockSpec((1, tokens, block), lambda j, ids: (j, 0, 0)),
                pl.BlockSpec((1, block, rank), lambda j, ids: (j, 0, 0)),
                pl.BlockSpec((1, 1, block), lambda j, ids: (j, 0, 0)),
                pl.BlockSpec((tokens, rank), lambda j, ids: (0, 0)),
                pl.BlockSpec((tokens, 1), lambda j, ids: (0, 0)),
                pl.BlockSpec((tokens, 1), lambda j, ids: (0, 0)),
            ],
            out_specs=pl.BlockSpec((tokens, block), lambda j, ids: (0, ids[j])),
        ),
        out_shape=jax.ShapeDtypeStruct((tokens, n * block), BF16),
        cost_estimate=pl.CostEstimate(
            flops=2 * tokens * n * block * rank, bytes_accessed=6 * tokens * n * block, transcendentals=0
        ),
        name="finish",
    )(ids, cot, x, down, gain, pre_grad, inverse, mean)


def gathered(routes, down, up, core):
    def send(block, route):
        return lax.ppermute(block, "dp", route)

    first = core == 0

    def of_chip(block):
        other = send(block, routes.partner)
        return jnp.where(first, jnp.concatenate([block, other]), jnp.concatenate([other, block]))

    downs, ups = {}, {}
    travelling = {}
    for slots, block, key in ((downs, down, "down"), (ups, up, "up")):
        travelling[key] = slots[0] = of_chip(block)
    for k in range(1, routes.half):
        for slots, key in ((downs, "down"), (ups, "up")):
            travelling[key] = slots[routes.behind(k)] = send(travelling[key], routes.onward)
            slots[routes.ahead(k)] = send(travelling[key], routes.partner)
    mine = send(jnp.where(first, travelling["down"], travelling["up"]), routes.onward)
    other = send(mine, routes.partner)
    downs[routes.opposite] = jnp.where(first, mine, other)
    ups[routes.opposite] = jnp.where(first, other, mine)
    return downs, ups


def scattered(routes, parts, core, far_core):
    def send(block, route):
        return lax.ppermute(block, "dp", route)

    opposite = parts[routes.opposite]
    to_far = [(a, b) for a, b in routes.partner if b % CORES == far_core]
    total = opposite.astype(F32) + send(opposite, to_far).astype(F32)
    total = send(total.astype(BF16), routes.onward_by_core[far_core]).astype(F32)
    for k in range(routes.half - 1, 0, -1):
        other = send(parts[routes.behind(k)], routes.partner).astype(F32)
        total = total + (other + parts[routes.ahead(k)].astype(F32))
        total = send(total.astype(BF16), routes.onward).astype(F32)
    total = total + parts[0].astype(F32)
    rows = total.shape[0] // CORES
    low, high = total[:rows], total[rows:]
    first = core == 0
    other = send(jnp.where(first, high, low).astype(BF16), routes.partner)
    return jnp.where(first, low, high) + other.astype(F32)


def local(section_inputs, teacher_states, confidence, gains, w_down, w_up):
    sections = lax.axis_size("section")
    devices = lax.axis_size("dp")
    section_index = lax.axis_index("section")
    dp_index = lax.axis_index("dp")
    core = dp_index % CORES
    is_last = section_index == sections - 1
    routes = Routes(devices)
    x = section_inputs[0]
    tokens, width = x.shape
    slots = range(routes.n)

    downs, ups = gathered(routes, w_down[0], w_up[0], core)

    ids = lax.dynamic_slice_in_dim(jnp.asarray(routes.table), dp_index, 1, 0)[0]
    values = x.astype(F32)
    inverse = lax.rsqrt(jnp.mean(values * values, axis=-1, keepdims=True) + EPSILON)
    x_slots, teacher_slots, scaled_slots, gain_slots = arrange(ids, x, teacher_states, gains, inverse)
    weight_rows = (confidence.astype(F32) / 256.0)[:, None]

    order = [0]
    for k in range(1, routes.half):
        order += [routes.behind(k), routes.ahead(k)]
    order.append(routes.opposite)
    preact = 0.0
    for j in order:
        preact = preact + jnp.dot(scaled_slots[j], downs[j], preferred_element_type=F32)
    hidden = jax.nn.silu(preact).astype(BF16)
    sigmoid_val = jax.nn.sigmoid(preact)
    slope = sigmoid_val * (1.0 + preact * (1.0 - sigmoid_val))

    def top_of(j):
        branch = jnp.einsum("tr,dr->td", hidden, ups[j], preferred_element_type=F32)
        return (weight_rows * (x_slots[j].astype(F32) + branch - teacher_slots[j].astype(F32))).astype(BF16)

    tops = {j: top_of(j) for j in order}
    leaving = order[::-1]

    def pre_grad_of(cots):
        hidden_grad = 0.0
        for j in leaving:
            hidden_grad = hidden_grad + jnp.dot(cots[j], ups[j], preferred_element_type=F32)
        pre_grad = (hidden_grad * slope).astype(BF16)
        mean = jnp.sum(pre_grad.astype(F32) * preact, axis=-1, keepdims=True) / width
        return pre_grad, mean

    def input_grad_of(j, cots, pre_grad, mean):
        grad = jnp.einsum("tr,dr->td", pre_grad, downs[j], preferred_element_type=F32)
        normed = x_slots[j].astype(F32) * inverse
        return (
            cots[j].astype(F32) + inverse * (grad * gain_slots[j] - normed * mean)
        ).astype(BF16)

    cots = tops
    back = [(s, s - 1) for s in range(1, sections)]
    for _ in range(sections - 1):
        pre_grad, mean = pre_grad_of(cots)
        arrived = {}
        for j in leaving:
            arrived[j] = lax.ppermute(input_grad_of(j, cots, pre_grad, mean), "section", back)
        cots = {j: jnp.where(is_last, tops[j], arrived[j]) for j in slots}

    def product(a, b):
        return lax.dot_general(a, b, (((0,), (0,)), ((), ())), preferred_element_type=F32).astype(BF16)

    up_sum = scattered(routes, {j: product(cots[j], hidden) for j in leaving}, core, 1)
    pre_grad, mean = pre_grad_of(cots)
    down_sum = scattered(routes, {j: product(scaled_slots[j], pre_grad) for j in leaving}, core, 0)
    input_grads = finish(
        ids,
        jnp.stack([cots[j] for j in slots]),
        x_slots,
        jnp.stack([downs[j] for j in slots]),
        gain_slots,
        pre_grad,
        inverse,
        mean,
    )
    grad_down = down_sum / tokens
    grad_up = up_sum / tokens
    own_gain = lax.dynamic_slice_in_dim(gains[0], dp_index * w_down.shape[1], w_down.shape[1], 0)
    grad_gain = jnp.sum(grad_down * w_down[0].astype(F32), axis=1) / own_gain
    return input_grads[None], grad_down[None], grad_up[None], grad_gain[None]


def solution(mesh):
    in_specs = (
        P("section", "dp", None),
        P("dp", None),
        P("dp"),
        P("section", None),
        P("section", "dp", None),
        P("section", "dp", None),
    )
    out_specs = (
        P("section", "dp", None),
        P("section", "dp", None),
        P("section", "dp", None),
        P("section", "dp"),
    )
    return jax.shard_map(local, mesh=mesh, in_specs=in_specs, out_specs=out_specs, check_vma=False)
```

```python
import jax
import jax.numpy as jnp
import numpy as np
from jax import lax
from jax.experimental import pallas as pl
from jax.experimental.pallas import tpu as pltpu
from jax.sharding import PartitionSpec as P

Z_CHIPS = 4
CORES = 2
EPSILON = 1e-05
F32 = jnp.float32
BF16 = jnp.bfloat16


def ring_of_chips(chips):
    rows = chips // Z_CHIPS
    cycle = []
    for z in range(Z_CHIPS):
        ys = range(1, rows) if z % 2 == 0 else range(rows - 1, 0, -1)
        cycle += [z * rows + y for y in ys]
    return cycle + [z * rows for z in range(Z_CHIPS - 1, -1, -1)]


class Routes:
    def __init__(self, devices):
        ring = ring_of_chips(devices // CORES)
        n = self.n = len(ring)
        half = self.half = n // 2
        self.partner = [(i, i ^ 1) for i in range(devices)]
        self.onward_by_core = [
            [(ring[i] * CORES + c, ring[(i + 1 - 2 * c) % n] * CORES + c) for i in range(n)] for c in range(CORES)
        ]
        self.onward = self.onward_by_core[0] + self.onward_by_core[1]
        steps = [0] + [-k for k in range(1, half)] + list(range(1, half)) + [half]
        self.table = np.zeros((devices, n), np.int32)
        for i, chip in enumerate(ring):
            for c in range(CORES):
                self.table[chip * CORES + c] = [ring[(i + (1 - 2 * c) * s) % n] for s in steps]
        self.opposite = n - 1

    def behind(self, k):
        return k

    def ahead(self, k):
        return self.half - 1 + k


def after(value, *earlier):
    return lax.optimization_barrier((value, *earlier))[0]


def arrange_inputs_kernel(ids, x_ref, gain_ref, inv_ref, x_out, scaled_out, gain_out):
    x = x_ref[...]
    x_out[0] = x
    gain = gain_ref[...]
    gain_out[0] = gain
    scaled_out[0] = ((x.astype(F32) * inv_ref[...]) * gain).astype(BF16)


def arrange_inputs(ids, x, gain, inverse):
    tokens, width = x.shape
    n = ids.shape[0]
    block = width // n
    by_slot = pl.BlockSpec((1, tokens, block), lambda j, ids: (j, 0, 0))
    return pl.pallas_call(
        arrange_inputs_kernel,
        grid_spec=pltpu.PrefetchScalarGridSpec(
            num_scalar_prefetch=1,
            grid=(n,),
            in_specs=[
                pl.BlockSpec((tokens, block), lambda j, ids: (0, ids[j])),
                pl.BlockSpec((1, block), lambda j, ids: (0, ids[j])),
                pl.BlockSpec((tokens, 1), lambda j, ids: (0, 0)),
            ],
            out_specs=[by_slot, by_slot, pl.BlockSpec((1, 1, block), lambda j, ids: (j, 0, 0))],
        ),
        out_shape=[
            jax.ShapeDtypeStruct((n, tokens, block), BF16),
            jax.ShapeDtypeStruct((n, tokens, block), BF16),
            jax.ShapeDtypeStruct((n, 1, block), F32),
        ],
        cost_estimate=pl.CostEstimate(flops=4 * tokens * width, bytes_accessed=6 * tokens * width, transcendentals=0),
        name="arrange_inputs",
    )(ids, x, gain, inverse)


def arrange_teacher_kernel(ids, t_ref, t_out):
    t_out[0] = t_ref[...]


def arrange_teacher(ids, teacher):
    tokens, width = teacher.shape
    n = ids.shape[0]
    block = width // n
    return pl.pallas_call(
        arrange_teacher_kernel,
        grid_spec=pltpu.PrefetchScalarGridSpec(
            num_scalar_prefetch=1,
            grid=(n,),
            in_specs=[pl.BlockSpec((tokens, block), lambda j, ids: (0, ids[j]))],
            out_specs=pl.BlockSpec((1, tokens, block), lambda j, ids: (j, 0, 0)),
        ),
        out_shape=jax.ShapeDtypeStruct((n, tokens, block), BF16),
        cost_estimate=pl.CostEstimate(flops=0, bytes_accessed=4 * tokens * width, transcendentals=0),
        name="arrange_teacher",
    )(ids, teacher)


def finish_kernel(ids, cot_ref, x_ref, down_ref, gain_ref, pre_ref, inv_ref, mean_ref, *rest):
    out_ref = rest[-1]
    grad = lax.dot_general(pre_ref[...], down_ref[...], (((1,), (1,)), ((), ())), preferred_element_type=F32)
    normed = x_ref[0].astype(F32) * inv_ref[...]
    out = cot_ref[...].astype(F32) + inv_ref[...] * (grad * gain_ref[0] - normed * mean_ref[...])
    out_ref[...] = out.astype(BF16)


def finish(ids, slot, cot, x_slots, down, gain_slots, pre_grad, inverse, mean, so_far):
    n, tokens, block = x_slots.shape
    rank = pre_grad.shape[1]

    def whole(*shape):
        return pl.BlockSpec(shape, lambda i, ids: (0,) * len(shape))

    given = [] if so_far is None else [so_far]
    return pl.pallas_call(
        finish_kernel,
        grid_spec=pltpu.PrefetchScalarGridSpec(
            num_scalar_prefetch=1,
            grid=(1,),
            in_specs=[
                whole(tokens, block),
                pl.BlockSpec((1, tokens, block), lambda i, ids: (slot, 0, 0)),
                whole(block, rank),
                pl.BlockSpec((1, 1, block), lambda i, ids: (slot, 0, 0)),
                whole(tokens, rank),
                whole(tokens, 1),
                whole(tokens, 1),
            ]
            + [pl.BlockSpec(memory_space=pl.ANY)] * len(given),
            out_specs=pl.BlockSpec((tokens, block), lambda i, ids: (0, ids[slot])),
        ),
        out_shape=jax.ShapeDtypeStruct((tokens, n * block), BF16),
        input_output_aliases={8: 0} if given else {},
        cost_estimate=pl.CostEstimate(
            flops=2 * tokens * block * rank, bytes_accessed=6 * tokens * block + 2 * block * rank, transcendentals=0
        ),
        name="finish",
    )(ids, cot, x_slots, down, gain_slots, pre_grad, inverse, mean, *given)


def local(section_inputs, teacher_states, confidence, gains, w_down, w_up):
    sections = lax.axis_size("section")
    devices = lax.axis_size("dp")
    section_index = lax.axis_index("section")
    dp_index = lax.axis_index("dp")
    first = dp_index % CORES == 0
    is_last = section_index == sections - 1
    routes = Routes(devices)
    half, opposite = routes.half, routes.opposite
    x = section_inputs[0]
    tokens, width = x.shape
    back = [(s, s - 1) for s in range(1, sections)]
    ahead_section = [(s, s + 1) for s in range(sections - 1)]

    def swap(block):
        return lax.ppermute(block, "dp", routes.partner)

    def onward(block):
        return lax.ppermute(block, "dp", routes.onward)

    def of_chip(own, other):
        return jnp.where(first, jnp.concatenate([own, other]), jnp.concatenate([other, own]))

    def own_half(block):
        rows = block.shape[0] // CORES
        return jnp.where(first, block[:rows], block[rows:])

    order = [0]
    for k in range(1, half):
        order += [routes.behind(k), routes.ahead(k)]
    order.append(opposite)
    leaving = [opposite]
    for k in range(half - 1, 0, -1):
        leaving += [routes.ahead(k), routes.behind(k)]
    leaving.append(0)

    downs, ups, next_ups = {}, {}, {}
    down, up = w_down[0], w_up[0]
    downs[0] = of_chip(down, swap(down))
    ups[0] = of_chip(up, swap(up))
    for k in range(1, half):
        downs[k] = onward(downs[k - 1])
        ups[k] = onward(ups[k - 1])
        downs[routes.ahead(k)] = swap(downs[k])
        ups[routes.ahead(k)] = swap(ups[k])
    down_far = onward(own_half(downs[half - 1]))
    up_far = onward(own_half(ups[half - 1]))
    downs[opposite] = of_chip(down_far, swap(down_far))
    ups[opposite] = of_chip(up_far, swap(up_far))

    relayed = {0: up}
    for k in range(1, half):
        relayed[k] = ups[k]
    relayed[opposite] = up_far
    for j, block in relayed.items():
        block = lax.ppermute(block, "section", ahead_section)
        other = swap(block)
        if j in (0, opposite):
            next_ups[j] = of_chip(block, other)
        else:
            next_ups[j], next_ups[routes.ahead(j)] = block, other

    values = x.astype(F32)
    inverse = lax.rsqrt(jnp.mean(values * values, axis=-1, keepdims=True) + EPSILON)
    table = after(jnp.asarray(routes.table), downs[0])
    ids = lax.dynamic_slice_in_dim(table, dp_index, 1, 0)[0]
    x_slots, scaled_slots, gain_slots = arrange_inputs(ids, after(x, downs[1]), gains, inverse)
    teacher_slots = arrange_teacher(ids, after(teacher_states, downs[2], scaled_slots))
    weight_rows = (confidence.astype(F32) / 256.0)[:, None]
    preact = 0.0
    for j in order:
        preact = preact + jnp.dot(scaled_slots[j], downs[j], preferred_element_type=F32)
    hidden = jax.nn.silu(preact).astype(BF16)
    sigmoid_val = jax.nn.sigmoid(preact)
    slope = sigmoid_val * (1.0 + preact * (1.0 - sigmoid_val))

    def top_of(j):
        branch = jnp.einsum("tr,dr->td", hidden, ups[j], preferred_element_type=F32)
        return (weight_rows * (x_slots[j].astype(F32) + branch - teacher_slots[j].astype(F32))).astype(BF16)

    tops = {j: top_of(j) for j in order}

    def through_rank(cots, matrices):
        total = 0.0
        for j in order:
            total = total + jnp.dot(cots[j], matrices[j], preferred_element_type=F32)
        return total

    def pre_grad_of(hidden_grad):
        pre_grad = (hidden_grad * slope).astype(BF16)
        return pre_grad, jnp.sum(pre_grad.astype(F32) * preact, axis=-1, keepdims=True) / width

    def input_grad_of(j, cot, pre_grad, mean):
        grad = jnp.einsum("tr,dr->td", pre_grad, downs[j], preferred_element_type=F32)
        normed = x_slots[j].astype(F32) * inverse
        return (cot.astype(F32) + inverse * (grad * gain_slots[j] - normed * mean)).astype(BF16)

    own_hidden_grad = through_rank(tops, ups)
    pre_grad, mean = pre_grad_of(own_hidden_grad)
    cots = tops
    for _ in range(sections - 1):
        sent = {j: input_grad_of(j, cots[j], pre_grad, mean) for j in leaving}
        next_hidden_grad = through_rank(sent, next_ups)
        arrived = {}
        queue = [sent[j] for j in leaving]
        queue.insert(2, next_hidden_grad)
        done = []
        for i, block in enumerate(queue):
            done.append(lax.ppermute(after(block, done[i - 2]) if i >= 2 else block, "section", back))
        hidden_grad = jnp.where(is_last, own_hidden_grad, done.pop(2))
        cots = {j: jnp.where(is_last, tops[j], block) for j, block in zip(leaving, done)}
        pre_grad, mean = pre_grad_of(hidden_grad)

    def scattered(parts, far_core):
        to_far = [(a, b) for a, b in routes.partner if b % CORES == far_core]
        total = parts[opposite].astype(F32) + lax.ppermute(parts[opposite], "dp", to_far).astype(F32)
        total = lax.ppermute(total.astype(BF16), "dp", routes.onward_by_core[far_core]).astype(F32)
        for k in range(half - 1, 0, -1):
            other = swap(parts[routes.behind(k)]).astype(F32)
            total = total + (other + parts[routes.ahead(k)].astype(F32))
            total = onward(total.astype(BF16)).astype(F32)
        total = total + parts[0].astype(F32)
        columns = total.shape[1] // CORES
        low, high = total[:, :columns], total[:, columns:]
        other = swap(jnp.where(first, high, low).astype(BF16))
        return (jnp.where(first, low, high) + other.astype(F32)).T / tokens

    def product(a, b):
        return jnp.dot(a, b, preferred_element_type=F32).astype(BF16)

    pre_t = lax.optimization_barrier(pre_grad.T)
    hidden_t = lax.optimization_barrier(hidden.T)
    grad_down = scattered({j: product(pre_t, scaled_slots[j]) for j in leaving}, 0)
    grad_up = scattered({j: product(hidden_t, cots[j]) for j in leaving}, 1)
    input_grads = None
    for j in leaving:
        input_grads = finish(ids, j, cots[j], x_slots, downs[j], gain_slots, pre_grad, inverse, mean, input_grads)
    own_gain = lax.dynamic_slice_in_dim(gains[0], dp_index * w_down.shape[1], w_down.shape[1], 0)
    grad_gain = jnp.sum(grad_down * down.astype(F32), axis=1) / own_gain
    return input_grads[None], grad_down[None], grad_up[None], grad_gain[None]


def solution(mesh):
    in_specs = (
        P("section", "dp", None),
        P("dp", None),
        P("dp"),
        P("section", None),
        P("section", "dp", None),
        P("section", "dp", None),
    )
    out_specs = (
        P("section", "dp", None),
        P("section", "dp", None),
        P("section", "dp", None),
        P("section", "dp"),
    )
    return jax.shard_map(local, mesh=mesh, in_specs=in_specs, out_specs=out_specs, check_vma=False)
```

```python
import functools

import jax
import jax.numpy as jnp
import numpy as np
from jax import lax
from jax.experimental import pallas as pl
from jax.experimental.pallas import tpu as pltpu
from jax.sharding import PartitionSpec as P

Z_CHIPS = 4
CORES = 2
EPSILON = 1e-05
F32 = jnp.float32
BF16 = jnp.bfloat16
VMEM = pl.BlockSpec(memory_space=pltpu.VMEM)
SMEM = pl.BlockSpec(memory_space=pltpu.SMEM)
ANY = pl.BlockSpec(memory_space=pl.ANY)
NT = (((1,), (1,)), ((), ()))


def ring_of_chips(chips):
    rows = chips // Z_CHIPS
    cycle = []
    for z in range(Z_CHIPS):
        ys = range(1, rows) if z % 2 == 0 else range(rows - 1, 0, -1)
        cycle += [z * rows + y for y in ys]
    return cycle + [z * rows for z in range(Z_CHIPS - 1, -1, -1)]


class Routes:
    def __init__(self, devices):
        ring = ring_of_chips(devices // CORES)
        n = self.n = len(ring)
        half = self.half = n // 2
        self.partner = [(i, i ^ 1) for i in range(devices)]
        self.onward = [
            (ring[i] * CORES + c, ring[(i + 1 - 2 * c) % n] * CORES + c) for c in range(CORES) for i in range(n)
        ]
        steps = [s for k in range(1, half) for s in (-k, k)] + [half, 0]
        self.table = np.zeros((devices, n), np.int32)
        for i, chip in enumerate(ring):
            for c in range(CORES):
                self.table[chip * CORES + c] = [ring[(i + (1 - 2 * c) * s) % n] for s in steps]
        self.opposite, self.own = n - 2, n - 1
        leaving = [self.opposite] + [f(k) for k in range(half - 1, 0, -1) for f in (self.ahead, self.behind)] + [self.own]
        self.groups = [leaving[:3], leaving[3:]]

    def behind(self, k):
        return 2 * k - 2

    def ahead(self, k):
        return 2 * k - 1


def after(value, *earlier):
    return lax.optimization_barrier((value, *earlier))[0] if earlier else value


def call(body, outs, *args, specs=None, out_specs=None, scratch=(), flops=0, aliases=None, vmem=8, name=None):
    single = not isinstance(outs, (list, tuple))
    outs = [outs] if single else list(outs)
    moved = sum(a.size * a.dtype.itemsize for a in args) + sum(o.size * o.dtype.itemsize for o in outs)
    result = pl.pallas_call(
        body,
        in_specs=specs or [VMEM] * len(args),
        out_specs=out_specs or [VMEM] * len(outs),
        out_shape=outs,
        scratch_shapes=scratch,
        input_output_aliases=aliases or {},
        cost_estimate=pl.CostEstimate(flops=flops, bytes_accessed=moved // 4, transcendentals=0),
        compiler_params=pltpu.CompilerParams(vmem_limit_bytes=vmem << 20),
        name=name,
    )(*args)
    return result[0] if single else result


class Place:
    def __init__(self, sections, table_ref):
        self.table, self.sections, self.n = table_ref, sections, table_ref.shape[1]

    def __getitem__(self, slot):
        return self.table[lax.axis_index("dp"), slot]

    def first(self):
        return lax.axis_index("dp") % CORES == 0

    def last(self):
        return lax.axis_index("section") == self.sections - 1


def placed(body, sections):
    def kernel(table_ref, *refs):
        body(Place(sections, table_ref), *refs)

    return kernel


def shape(dtype, *dims):
    return jax.ShapeDtypeStruct(dims, dtype)


def columns(ref, chip, block):
    return ref[:, pl.ds(pl.multiple_of(chip * block, block), block)]


def scale_kernel(block, x_ref, gain_ref, conf_ref, down_ref, inv_ref, scaled_ref, weight_ref, down_t_ref):
    tokens, width = x_ref.shape
    squares = jnp.zeros((tokens, block), F32)
    for at in range(0, width, block):
        values = x_ref[:, at : at + block].astype(F32)
        squares = squares + values * values
    inverse = lax.rsqrt(jnp.sum(squares, axis=-1, keepdims=True) / width + EPSILON)
    inv_ref[...] = inverse
    for at in range(0, width, block):
        values = x_ref[:, at : at + block].astype(F32)
        scaled_ref[:, at : at + block] = ((values * inverse) * gain_ref[:, at : at + block]).astype(BF16)
    weights = jnp.broadcast_to(conf_ref[...].astype(F32) / 256.0, (tokens, tokens))
    row = lax.broadcasted_iota(jnp.int32, (tokens, tokens), 0)
    column = lax.broadcasted_iota(jnp.int32, (tokens, tokens), 1)
    weight_ref[...] = jnp.sum(jnp.where(row == column, weights, 0.0), axis=1, keepdims=True)
    down_t_ref[...] = down_ref[...].astype(F32).T


def fetch(sources, held, sems):
    copies = [pltpu.make_async_copy(ref, held.at[i], sems.at[i]) for i, ref in enumerate(sources)]
    for copy in copies:
        copy.start()
    return copies


def assemble_kernel(mine_ref, other_ref, out_ref, sems):
    rows = mine_ref.shape[0]
    core = lax.axis_index("dp") % CORES
    copies = []
    for i, (ref, place) in enumerate(((mine_ref, core), (other_ref, 1 - core))):
        out = out_ref.at[pl.ds(pl.multiple_of(place * rows, rows), rows)]
        copies.append(pltpu.make_async_copy(ref, out, sems.at[i]))
        copies[-1].start()
    for copy in copies:
        copy.wait()


def pick_kernel(zero_ref, one_ref, out_ref, sem):
    core = lax.axis_index("dp") % CORES
    for at, ref in enumerate((zero_ref, one_ref)):

        @pl.when(core == at)
        def _():
            copy = pltpu.make_async_copy(ref, out_ref, sem)
            copy.start()
            copy.wait()


def pre_grad_of(hidden_grad, slope, preact, width):
    pre_grad = (hidden_grad * slope).astype(BF16)
    return pre_grad, jnp.sum(pre_grad.astype(F32) * preact, axis=-1, keepdims=True) / width


def top_kernel(groups, meta, x_ref, t_ref, scaled_ref, weight_ref, *refs):
    n = meta.n
    held, held_x, sems, sems_x = refs[-4:]
    pre_out, mean_out, hid_out, slope_out, preact_out, sum_out, *tops = refs[2 * n : -4]
    width = x_ref.shape[1]
    block = width // n
    order = [slot for group in groups for slot in group]
    copies = fetch(refs[: 2 * n], held, sems)
    x_copies = {}
    for i, slot in enumerate(order):
        place = pl.ds(pl.multiple_of(meta[slot] * block, block), block)
        for at, ref in enumerate((x_ref, t_ref)):
            x_copies[i, at] = pltpu.make_async_copy(ref.at[:, place], held_x.at[i, at], sems_x.at[i, at])
            x_copies[i, at].start()
    preact = jnp.zeros(preact_out.shape, F32)
    for slot in range(n):
        copies[slot].wait()
        preact = preact + jnp.dot(columns(scaled_ref, meta[slot], block), held[slot], preferred_element_type=F32)
    sigmoid_val = 1.0 / (1.0 + jnp.exp(-preact))
    slope = sigmoid_val * (1.0 + preact * (1.0 - sigmoid_val))
    hidden = preact * sigmoid_val
    preact_out[...] = preact
    slope_out[...] = slope
    hid_out[...] = hidden.T.astype(BF16)
    hidden = hidden.astype(BF16)
    weight = weight_ref[...]
    total = jnp.zeros_like(preact)
    i = 0
    for group, top_ref in zip(groups, tops):
        for at, slot in enumerate(group):
            copies[n + slot].wait()
            branch = lax.dot_general(hidden, held[n + slot], NT, preferred_element_type=F32)
            x_copies[i, 0].wait()
            x_copies[i, 1].wait()
            values = held_x[i, 0].astype(F32) + branch - held_x[i, 1].astype(F32)
            top = (weight * values).astype(BF16)
            top_ref[at] = top
            total = total + jnp.dot(top, held[n + slot], preferred_element_type=F32)
            i += 1
    sum_out[...] = total
    pre_out[...], mean_out[...] = pre_grad_of(total, slope, preact, width)


def input_grad(cot, x, down, gain, pre_grad, inverse, mean):
    grad = lax.dot_general(pre_grad, down, NT, preferred_element_type=F32)
    return (cot.astype(F32) + inverse * (grad * gain - x.astype(F32) * inverse * mean)).astype(BF16)


def leave_kernel(slots, meta, cot_ref, x_ref, gain_ref, pre_ref, inv_ref, mean_ref, *refs):
    downs, out_ref = refs[:-1], refs[-1]
    for at, slot in enumerate(slots):
        block = downs[at].shape[0]
        x, gain = columns(x_ref, meta[slot], block), columns(gain_ref, meta[slot], block)
        out_ref[at] = input_grad(cot_ref[at], x, downs[at][...], gain, pre_ref[...], inv_ref[...], mean_ref[...])


def arrive_kernel(follows, meta, arrived_ref, top_ref, hid_ref, *refs):
    count = arrived_ref.shape[0]
    total = refs[0][...] if follows else 0.0
    refs = refs[1:] if follows else refs
    ups, (cot_ref, sum_out, *parts) = refs[:count], refs[count:]
    for at in range(count):
        cot = jnp.where(meta.last(), top_ref[at], arrived_ref[at])
        cot_ref[at] = cot
        parts[at][...] = jnp.dot(hid_ref[...], cot, preferred_element_type=F32).astype(BF16)
        total = total + jnp.dot(cot, ups[at][...], preferred_element_type=F32)
    sum_out[...] = total


def pre_grad_kernel(width, sum_ref, slope_ref, preact_ref, pre_out, pre_t_out, mean_out):
    hidden_grad = sum_ref[...]
    slope = slope_ref[...]
    pre_out[...], mean_out[...] = pre_grad_of(hidden_grad, slope, preact_ref[...], width)
    pre_t_out[...] = (hidden_grad * slope).T.astype(BF16)


def products_kernel(slots, stacked, meta, scaled_ref, pre_t_ref, *outs):
    block = outs[0].shape[-1]
    for at, slot in enumerate(slots):
        part = jnp.dot(pre_t_ref[...], columns(scaled_ref, meta[slot], block), preferred_element_type=F32)
        if stacked:
            outs[0][at] = part.astype(BF16)
        else:
            outs[at][...] = part.astype(BF16)


def add_kernel(picks, *refs):
    out_ref = refs[-1]
    total = None
    for ref, pick in zip(refs[:-1], picks):
        value = (ref[...] if pick is None else ref[pick]).astype(F32)
        total = value if total is None else total + value
    out_ref[...] = total.astype(out_ref.dtype)


def add(out, *terms):
    arrays = [t[0] if isinstance(t, tuple) else t for t in terms]
    picks = [t[1] if isinstance(t, tuple) else None for t in terms]
    return call(functools.partial(add_kernel, picks), out, *arrays, name="add")


def split_kernel(meta, total_ref, part_ref, mine_ref, other_ref):
    half = mine_ref.shape[1]
    first = meta.first()
    low = total_ref[:, :half].astype(F32) + part_ref[:, :half].astype(F32)
    high = total_ref[:, half:].astype(F32) + part_ref[:, half:].astype(F32)
    mine_ref[...] = jnp.where(first, low, high)
    other_ref[...] = jnp.where(first, high, low).astype(BF16)


def close_kernel(tokens, mine_ref, other_ref, grad_ref):
    grad_ref[0] = ((mine_ref[...] + other_ref[...].astype(F32)) / tokens).T


def close_gain_kernel(tokens, meta, mine_ref, other_ref, down_t_ref, gain_ref, grad_ref, gain_grad_ref):
    grad = (mine_ref[...] + other_ref[...].astype(F32)) / tokens
    grad_ref[0] = grad.T
    columns_own = grad.shape[1]
    gain = columns(gain_ref, lax.axis_index("dp"), columns_own)
    gain_grad_ref[...] = jnp.sum(grad * down_t_ref[...], axis=0, keepdims=True) / gain


def finish_kernel(groups, meta, x_ref, gain_ref, pre_ref, inv_ref, mean_ref, *refs):
    slots = [slot for group in groups for slot in group]
    downs, cots = refs[: len(slots)], refs[len(slots) : len(slots) + len(groups)]
    out_ref, held, sems = refs[-3:]
    copies = []
    for group, cot_ref in zip(groups, cots):
        for at, slot in enumerate(group):
            i = len(copies)
            down = downs[i][...]
            block = down.shape[0]
            chip = meta[slot]
            x, gain = columns(x_ref, chip, block), columns(gain_ref, chip, block)
            held[i] = input_grad(cot_ref[at], x, down, gain, pre_ref[...], inv_ref[...], mean_ref[...])
            place = out_ref.at[:, pl.ds(pl.multiple_of(chip * block, block), block)]
            copies.append(pltpu.make_async_copy(held.at[i], place, sems.at[i]))
            copies[-1].start()
    for copy in copies:
        copy.wait()


def local(section_inputs, teacher_states, confidence, gains, w_down, w_up):
    sections = lax.axis_size("section")
    devices = lax.axis_size("dp")
    routes = Routes(devices)
    n, half, opposite, own, groups = routes.n, routes.half, routes.opposite, routes.own, routes.groups
    behind, ahead = routes.behind, routes.ahead
    x = section_inputs[0]
    tokens, width = x.shape
    block = width // n
    rank = w_down.shape[2]
    half_block = block // CORES
    back = [(s, s - 1) for s in range(1, sections)]
    groups_of = [range(0, 1), range(1, 2)]

    def swap(value):
        return lax.ppermute(value, "dp", routes.partner)

    def onward(value):
        return lax.ppermute(value, "dp", routes.onward)

    chunk, part_shape = shape(BF16, block, rank), shape(BF16, rank, block)

    def of_chip(mine, other):
        return call(
            assemble_kernel, chunk, mine, other, specs=[ANY] * 2, scratch=[pltpu.SemaphoreType.DMA((2,))], name="assemble"
        )

    def pick(zero, one):
        return call(pick_kernel, chunk, zero, one, specs=[ANY] * 2, scratch=[pltpu.SemaphoreType.DMA], name="pick")

    down, up = w_down[0], w_up[0]
    downs, ups = {}, {}
    downs[own] = of_chip(down, swap(down))
    ups[own] = of_chip(up, swap(up))
    table = jnp.asarray(routes.table)

    def with_meta(body, outs, *args, **kw):
        specs = [SMEM] + kw.pop("specs", [VMEM] * len(args))
        return call(placed(body, sections), outs, table, *args, specs=specs, **kw)

    inverse, scaled, weight_rows, down_t = call(
        functools.partial(scale_kernel, block),
        [shape(F32, tokens, 1), shape(BF16, tokens, width), shape(F32, tokens, 1), shape(F32, rank, half_block)],
        after(x, downs[own]), gains, confidence[None], down, name="scale",
    )
    down_block, up_block = downs[own], after(ups[own], scaled)
    for k in range(1, half):
        earlier = [downs[ahead(k - 2)], ups[ahead(k - 2)]] if k >= 3 else []
        downs[behind(k)] = down_block = onward(after(down_block, *earlier))
        ups[behind(k)] = up_block = onward(up_block)
        downs[ahead(k)] = swap(down_block)
        ups[ahead(k)] = swap(up_block)
    earlier = [downs[ahead(half - 2)], ups[ahead(half - 2)]] if half >= 3 else []
    mine = onward(after(pick(down_block, up_block), *earlier))
    other = swap(mine)
    downs[opposite], ups[opposite] = pick(mine, other), pick(other, mine)

    rank_f32, rank_bf16 = shape(F32, tokens, rank), shape(BF16, tokens, rank)
    pre_grad, mean, hidden_t, slope, preact, own_sum, *tops = with_meta(
        functools.partial(top_kernel, groups),
        [rank_bf16, shape(F32, tokens, 1), shape(BF16, rank, tokens), rank_f32, rank_f32, rank_f32]
        + [shape(BF16, len(slots), tokens, block) for slots in groups],
        x, teacher_states, scaled, weight_rows, *(downs[j] for j in range(n)), *(ups[j] for j in range(n)),
        specs=[ANY] * 2 + [VMEM] * 2 + [ANY] * (2 * n),
        scratch=[
            pltpu.VMEM((2 * n, block, rank), BF16),
            pltpu.VMEM((n, 2, tokens, block), BF16),
            pltpu.SemaphoreType.DMA((2 * n,)),
            pltpu.SemaphoreType.DMA((n, 2)),
        ],
        flops=6 * tokens * width * rank, vmem=24, name="top",
    )

    def leave(slots, cot, pre_grad, mean):
        return with_meta(
            functools.partial(leave_kernel, slots), shape(BF16, len(slots), tokens, block),
            cot, x, gains, pre_grad, inverse, mean, *(downs[j] for j in slots),
            flops=2 * len(slots) * tokens * block * rank, name="leave",
        )

    def arrive(slots, value, top, total):
        cot, total, *parts = with_meta(
            functools.partial(arrive_kernel, total is not None),
            [shape(BF16, *value.shape), rank_f32] + [part_shape] * len(slots),
            value, top, hidden_t, *([] if total is None else [total]), *(ups[j] for j in slots),
            flops=4 * len(slots) * tokens * block * rank, name="arrive",
        )
        return cot, parts, total

    def rank_grad(total):
        return call(
            functools.partial(pre_grad_kernel, width),
            [rank_bf16, shape(BF16, rank, tokens), shape(F32, tokens, 1)],
            total, slope, preact, name="pre_grad",
        )


    def split(total, part):
        return with_meta(
            split_kernel, [shape(F32, rank, half_block), shape(BF16, rank, half_block)],
            total, part, name="split",
        )

    cots = tops
    for hop in range(sections - 1):
        sent = [leave(slots, cot, pre_grad, mean) for slots, cot in zip(groups, cots)]
        if hop < sections - 2:
            arrived, cots = [], []
            hidden_grad = None
            for i, value in enumerate(sent):
                arrived.append(lax.ppermute(after(value, *arrived[i - 2 : i - 1] if i >= 2 else ()), "section", back))
                cot, _, hidden_grad = arrive(groups[i], arrived[i], tops[i], hidden_grad)
                cots.append(cot)
            pre_grad, _, mean = rank_grad(hidden_grad)

    arrived = [lax.ppermute(value, "section", back) for value in sent]
    near_cot, parts, hidden_grad = arrive(groups[0], after(arrived[0], sent[1]), tops[0], None)
    total = onward(parts[0])
    total = onward(add(part_shape, total, parts[1], swap(parts[2])))
    cot, parts, hidden_grad = arrive(groups[1], after(arrived[1], total), tops[1], hidden_grad)
    cots = [near_cot, cot]
    for k in range(half - 2, 0, -1):
        at = 2 * (half - 2 - k)
        total = onward(add(part_shape, total, parts[at], swap(parts[at + 1])))
    up_mine, up_other = split(total, parts[-1])
    up_other = swap(up_other)
    grad_up = call(
        functools.partial(close_kernel, tokens), shape(F32, 1, half_block, rank), up_mine, up_other, name="close_up"
    )

    pre_grad, pre_t, mean = rank_grad(hidden_grad)

    def products(slots, stacked=False):
        return with_meta(
            functools.partial(products_kernel, slots, stacked),
            shape(BF16, len(slots), rank, block) if stacked else [part_shape] * len(slots), scaled, pre_t,
            flops=2 * len(slots) * tokens * block * rank, name="products",
        )

    (far,) = products([opposite])
    total = onward(far)
    behinds = products([behind(k) for k in range(1, half)], stacked=True)
    aheads = products([ahead(k) for k in range(1, half)])
    swapped = swap(behinds)

    def finish(some, so_far):
        slots = [j for i in some for j in groups[i]]
        args = [x, gains, pre_grad, inverse, mean, *(downs[j] for j in slots), *(cots[i] for i in some)]
        given = [] if so_far is None else [so_far]
        return with_meta(
            functools.partial(finish_kernel, [groups[i] for i in some]), shape(BF16, tokens, width), *args, *given,
            specs=[VMEM] * len(args) + [ANY] * len(given), out_specs=[ANY],
            scratch=[pltpu.VMEM((len(slots), tokens, block), BF16), pltpu.SemaphoreType.DMA((len(slots),))],
            aliases={len(args) + 1: 0} if given else {},
            flops=2 * len(slots) * tokens * block * rank, name="finish",
        )

    (mine,) = products([own])
    input_grads = finish(groups_of[0], None)
    for at, k in enumerate(range(half - 1, 0, -1)):
        part, other = aheads[k - 1], (swapped, k - 1)
        if at >= 1 and at < len(groups_of):
            input_grads = finish(groups_of[at], input_grads)
        total = after(total, input_grads)
        total = onward(add(part_shape, total, part, other))
    down_mine, down_other = split(total, mine)
    down_other = swap(down_other)
    grad_down, grad_gain = with_meta(
        functools.partial(close_gain_kernel, tokens),
        [shape(F32, 1, half_block, rank), shape(F32, 1, half_block)],
        down_mine, down_other, down_t, gains, name="close_down",
    )
    return input_grads[None], grad_down, grad_up, grad_gain


def solution(mesh):
    in_specs = (
        P("section", "dp", None),
        P("dp", None),
        P("dp"),
        P("section", None),
        P("section", "dp", None),
        P("section", "dp", None),
    )
    out_specs = (
        P("section", "dp", None),
        P("section", "dp", None),
        P("section", "dp", None),
        P("section", "dp"),
    )
    return jax.shard_map(local, mesh=mesh, in_specs=in_specs, out_specs=out_specs, check_vma=False)
```

```python
import functools

import jax
import jax.numpy as jnp
import numpy as np
from jax import lax
from jax.experimental import pallas as pl
from jax.experimental.pallas import tpu as pltpu
from jax.sharding import PartitionSpec as P

Z_CHIPS = 4
CORES = 2
EPSILON = 1e-05
F32 = jnp.float32
BF16 = jnp.bfloat16
VMEM = pl.BlockSpec(memory_space=pltpu.VMEM)
SMEM = pl.BlockSpec(memory_space=pltpu.SMEM)
ANY = pl.BlockSpec(memory_space=pl.ANY)
NT = (((1,), (1,)), ((), ()))


def ring_of_chips(chips):
    rows = chips // Z_CHIPS
    cycle = []
    for z in range(Z_CHIPS):
        ys = range(1, rows) if z % 2 == 0 else range(rows - 1, 0, -1)
        cycle += [z * rows + y for y in ys]
    return cycle + [z * rows for z in range(Z_CHIPS - 1, -1, -1)]


class Routes:
    def __init__(self, devices):
        ring = ring_of_chips(devices // CORES)
        n = self.n = len(ring)
        half = self.half = n // 2
        self.partner = [(i, i ^ 1) for i in range(devices)]
        self.onward = [
            (ring[i] * CORES + c, ring[(i + 1 - 2 * c) % n] * CORES + c) for c in range(CORES) for i in range(n)
        ]
        steps = [s for k in range(1, half) for s in (-k, k)] + [half, 0]
        self.table = np.zeros((devices, n), np.int32)
        for i, chip in enumerate(ring):
            for c in range(CORES):
                self.table[chip * CORES + c] = [ring[(i + (1 - 2 * c) * s) % n] for s in steps]
        self.opposite, self.own = n - 2, n - 1
        leaving = [self.opposite] + [f(k) for k in range(half - 1, 0, -1) for f in (self.ahead, self.behind)] + [self.own]
        self.groups = [leaving[:3], leaving[3:]]

    def behind(self, k):
        return 2 * k - 2

    def ahead(self, k):
        return 2 * k - 1


def after(value, *earlier):
    return lax.optimization_barrier((value, *earlier))[0] if earlier else value


def call(body, outs, *args, specs=None, out_specs=None, scratch=(), flops=0, aliases=None, vmem=8, name=None):
    single = not isinstance(outs, (list, tuple))
    outs = [outs] if single else list(outs)
    moved = sum(a.size * a.dtype.itemsize for a in args) + sum(o.size * o.dtype.itemsize for o in outs)
    result = pl.pallas_call(
        body,
        in_specs=specs or [VMEM] * len(args),
        out_specs=out_specs or [VMEM] * len(outs),
        out_shape=outs,
        scratch_shapes=scratch,
        input_output_aliases=aliases or {},
        cost_estimate=pl.CostEstimate(flops=flops, bytes_accessed=moved // 4, transcendentals=0),
        compiler_params=pltpu.CompilerParams(vmem_limit_bytes=vmem << 20),
        name=name,
    )(*args)
    return result[0] if single else result


class Place:
    def __init__(self, sections, table_ref):
        self.table, self.sections, self.n = table_ref, sections, table_ref.shape[1]

    def __getitem__(self, slot):
        return self.table[lax.axis_index("dp"), slot]

    def first(self):
        return lax.axis_index("dp") % CORES == 0

    def last(self):
        return lax.axis_index("section") == self.sections - 1


def placed(body, sections):
    def kernel(table_ref, *refs):
        body(Place(sections, table_ref), *refs)

    return kernel


def shape(dtype, *dims):
    return jax.ShapeDtypeStruct(dims, dtype)


def columns(ref, chip, block):
    return ref[:, pl.ds(pl.multiple_of(chip * block, block), block)]


def scale_kernel(block, x_ref, gain_ref, conf_ref, down_ref, inv_ref, scaled_ref, weight_ref, down_t_ref):
    tokens, width = x_ref.shape
    squares = jnp.zeros((tokens, block), F32)
    for at in range(0, width, block):
        values = x_ref[:, at : at + block].astype(F32)
        squares = squares + values * values
    inverse = lax.rsqrt(jnp.sum(squares, axis=-1, keepdims=True) / width + EPSILON)
    inv_ref[...] = inverse
    for at in range(0, width, block):
        values = x_ref[:, at : at + block].astype(F32)
        scaled_ref[:, at : at + block] = ((values * inverse) * gain_ref[:, at : at + block]).astype(BF16)
    weights = jnp.broadcast_to(conf_ref[...].astype(F32) / 256.0, (tokens, tokens))
    row = lax.broadcasted_iota(jnp.int32, (tokens, tokens), 0)
    column = lax.broadcasted_iota(jnp.int32, (tokens, tokens), 1)
    weight_ref[...] = jnp.sum(jnp.where(row == column, weights, 0.0), axis=1, keepdims=True)
    down_t_ref[...] = down_ref[...].astype(F32).T


def assemble_kernel(mine_ref, other_ref, out_ref, sems):
    rows = mine_ref.shape[0]
    core = lax.axis_index("dp") % CORES
    copies = []
    for i, (ref, place) in enumerate(((mine_ref, core), (other_ref, 1 - core))):
        out = out_ref.at[pl.ds(pl.multiple_of(place * rows, rows), rows)]
        copies.append(pltpu.make_async_copy(ref, out, sems.at[i]))
        copies[-1].start()
    for copy in copies:
        copy.wait()


def pick_kernel(zero_ref, one_ref, out_ref, sem):
    core = lax.axis_index("dp") % CORES
    for at, ref in enumerate((zero_ref, one_ref)):

        @pl.when(core == at)
        def _():
            copy = pltpu.make_async_copy(ref, out_ref, sem)
            copy.start()
            copy.wait()


def pre_grad_of(hidden_grad, slope, preact, width):
    pre_grad = (hidden_grad * slope).astype(BF16)
    return pre_grad, jnp.sum(pre_grad.astype(F32) * preact, axis=-1, keepdims=True) / width


def preact_kernel(slots, meta, scaled_ref, *refs):
    downs, out_ref = refs[:-1], refs[-1]
    total = 0.0
    for slot, down_ref in zip(slots, downs):
        scaled = columns(scaled_ref, meta[slot], down_ref.shape[0])
        total = total + jnp.dot(scaled, down_ref[...], preferred_element_type=F32)
    out_ref[...] = total


def top_kernel(groups, opposite, meta, x_ref, t_ref, scaled_ref, weight_ref, sum_ref, down_ref, *refs):
    n = meta.n
    ups, (pre_out, mean_out, hid_out, slope_out, preact_out, sum_out, *tops) = refs[:n], refs[n:]
    width = x_ref.shape[1]
    block = width // n
    far = columns(scaled_ref, meta[opposite], block)
    preact = sum_ref[...] + jnp.dot(far, down_ref[...], preferred_element_type=F32)
    sigmoid_val = 1.0 / (1.0 + jnp.exp(-preact))
    slope = sigmoid_val * (1.0 + preact * (1.0 - sigmoid_val))
    hidden = preact * sigmoid_val
    preact_out[...] = preact
    slope_out[...] = slope
    hid_out[...] = hidden.T.astype(BF16)
    hidden = hidden.astype(BF16)
    weight = weight_ref[...]
    total = jnp.zeros_like(preact)
    for group, top_ref in zip(groups, tops):
        for at, slot in enumerate(group):
            branch = lax.dot_general(hidden, ups[slot][...], NT, preferred_element_type=F32)
            chip = meta[slot]
            values = columns(x_ref, chip, block).astype(F32) + branch - columns(t_ref, chip, block).astype(F32)
            top = (weight * values).astype(BF16)
            top_ref[at] = top
            total = total + jnp.dot(top, ups[slot][...], preferred_element_type=F32)
    sum_out[...] = total
    pre_out[...], mean_out[...] = pre_grad_of(total, slope, preact, width)


def input_grad(cot, x, down, gain, pre_grad, inverse, mean):
    grad = lax.dot_general(pre_grad, down, NT, preferred_element_type=F32)
    return (cot.astype(F32) + inverse * (grad * gain - x.astype(F32) * inverse * mean)).astype(BF16)


def leave_kernel(slots, meta, cot_ref, x_ref, gain_ref, pre_ref, inv_ref, mean_ref, *refs):
    downs, out_ref = refs[:-1], refs[-1]
    for at, slot in enumerate(slots):
        block = downs[at].shape[0]
        x, gain = columns(x_ref, meta[slot], block), columns(gain_ref, meta[slot], block)
        out_ref[at] = input_grad(cot_ref[at], x, downs[at][...], gain, pre_ref[...], inv_ref[...], mean_ref[...])


def arrive_kernel(follows, width, opposite, meta, arrived_ref, top_ref, hid_ref, *refs):
    count = arrived_ref.shape[0]
    ups, refs = refs[:count], refs[count:]
    total = 0.0
    if follows:
        sum_ref, slope_ref, preact_ref, scaled_ref, cot_ref, pre_out, pre_t_out, mean_out, *outs = refs
        total = sum_ref[...]
        outs, parts = outs[:2], outs[2:]
    else:
        cot_ref, sum_out, *parts = refs
    for at in range(count):
        cot = jnp.where(meta.last(), top_ref[at], arrived_ref[at])
        cot_ref[at] = cot
        total = total + jnp.dot(cot, ups[at][...], preferred_element_type=F32)
        parts[at][...] = jnp.dot(hid_ref[...], cot, preferred_element_type=F32).astype(BF16)
    if not follows:
        sum_out[...] = total
        return
    pre_out[...], mean_out[...] = pre_grad_of(total, slope_ref[...], preact_ref[...], width)
    pre_t = (total * slope_ref[...]).T.astype(BF16)
    pre_t_out[...] = pre_t
    put_product(pre_t, columns(scaled_ref, meta[opposite], ups[0].shape[0]), outs)


def put_product(pre_t, scaled, halves):
    part = jnp.dot(pre_t, scaled, preferred_element_type=F32).astype(BF16)
    half = part.shape[1] // 2
    halves[0][...] = part[:, :half]
    halves[1][...] = part[:, half:]


def products_kernel(slots, meta, scaled_ref, pre_t_ref, *outs):
    for at, slot in enumerate(slots):
        halves = outs[2 * at : 2 * at + 2]
        put_product(pre_t_ref[...], columns(scaled_ref, meta[slot], 2 * halves[0].shape[1]), halves)


def stack_kernel(slots, meta, scaled_ref, pre_t_ref, out_ref):
    for at, slot in enumerate(slots):
        halves = out_ref.at[2 * at], out_ref.at[2 * at + 1]
        put_product(pre_t_ref[...], columns(scaled_ref, meta[slot], 2 * out_ref.shape[2]), halves)


def add_kernel(picks, *refs):
    out_ref = refs[-1]
    total = None
    for ref, pick in zip(refs[:-1], picks):
        value = (ref[...] if pick is None else ref[pick]).astype(F32)
        total = value if total is None else total + value
    out_ref[...] = total.astype(out_ref.dtype)


def add(out, *terms):
    arrays = [t[0] if isinstance(t, tuple) else t for t in terms]
    picks = [t[1] if isinstance(t, tuple) else None for t in terms]
    return call(functools.partial(add_kernel, picks), out, *arrays, name="add")


def split_kernel(meta, total_ref, part_ref, mine_ref, other_ref):
    half = mine_ref.shape[1]
    first = meta.first()
    low = total_ref[:, :half].astype(F32) + part_ref[:, :half].astype(F32)
    high = total_ref[:, half:].astype(F32) + part_ref[:, half:].astype(F32)
    mine_ref[...] = jnp.where(first, low, high)
    other_ref[...] = jnp.where(first, high, low).astype(BF16)


def split_halves_kernel(meta, low_ref, high_ref, low_part, high_part, mine_ref, other_ref):
    first = meta.first()
    low = low_ref[...].astype(F32) + low_part[...].astype(F32)
    high = high_ref[...].astype(F32) + high_part[...].astype(F32)
    mine_ref[...] = jnp.where(first, low, high)
    other_ref[...] = jnp.where(first, high, low).astype(BF16)


def close_kernel(tokens, mine_ref, other_ref, grad_ref):
    grad_ref[0] = ((mine_ref[...] + other_ref[...].astype(F32)) / tokens).T


def close_gain_kernel(tokens, meta, mine_ref, other_ref, down_t_ref, gain_ref, grad_ref, gain_grad_ref):
    grad = (mine_ref[...] + other_ref[...].astype(F32)) / tokens
    grad_ref[0] = grad.T
    columns_own = grad.shape[1]
    gain = columns(gain_ref, lax.axis_index("dp"), columns_own)
    gain_grad_ref[...] = jnp.sum(grad * down_t_ref[...], axis=0, keepdims=True) / gain


def finish_kernel(groups, meta, x_ref, gain_ref, pre_ref, inv_ref, mean_ref, *refs):
    slots = [slot for group in groups for slot in group]
    downs, cots = refs[: len(slots)], refs[len(slots) : len(slots) + len(groups)]
    out_ref, held, sems = refs[-3:]
    copies = []
    for group, cot_ref in zip(groups, cots):
        for at, slot in enumerate(group):
            i = len(copies)
            down = downs[i][...]
            block = down.shape[0]
            chip = meta[slot]
            x, gain = columns(x_ref, chip, block), columns(gain_ref, chip, block)
            held[i] = input_grad(cot_ref[at], x, down, gain, pre_ref[...], inv_ref[...], mean_ref[...])
            place = out_ref.at[:, pl.ds(pl.multiple_of(chip * block, block), block)]
            copies.append(pltpu.make_async_copy(held.at[i], place, sems.at[i]))
            copies[-1].start()
    for copy in copies:
        copy.wait()


def local(section_inputs, teacher_states, confidence, gains, w_down, w_up):
    sections = lax.axis_size("section")
    devices = lax.axis_size("dp")
    routes = Routes(devices)
    n, half, opposite, own, groups = routes.n, routes.half, routes.opposite, routes.own, routes.groups
    behind, ahead = routes.behind, routes.ahead
    x = section_inputs[0]
    tokens, width = x.shape
    block = width // n
    rank = w_down.shape[2]
    half_block = block // CORES
    back = [(s, s - 1) for s in range(1, sections)]

    def swap(value):
        return lax.ppermute(value, "dp", routes.partner)

    def onward(value):
        return lax.ppermute(value, "dp", routes.onward)

    rank_f32, rank_bf16 = shape(F32, tokens, rank), shape(BF16, tokens, rank)
    half_part = shape(BF16, rank, block // CORES)
    chunk, part_shape = shape(BF16, block, rank), shape(BF16, rank, block)

    def of_chip(mine, other):
        return call(
            assemble_kernel, chunk, mine, other, specs=[ANY] * 2, scratch=[pltpu.SemaphoreType.DMA((2,))], name="assemble"
        )

    def pick(zero, one):
        return call(pick_kernel, chunk, zero, one, specs=[ANY] * 2, scratch=[pltpu.SemaphoreType.DMA], name="pick")

    down, up = w_down[0], w_up[0]
    downs, ups = {}, {}
    downs[own] = of_chip(down, swap(down))
    ups[own] = of_chip(up, swap(up))
    table = jnp.asarray(routes.table)

    def with_meta(body, outs, *args, **kw):
        specs = [SMEM] + kw.pop("specs", [VMEM] * len(args))
        return call(placed(body, sections), outs, table, *args, specs=specs, **kw)

    inverse, scaled, weight_rows, down_t = call(
        functools.partial(scale_kernel, block),
        [shape(F32, tokens, 1), shape(BF16, tokens, width), shape(F32, tokens, 1), shape(F32, rank, half_block)],
        after(x, downs[own]), gains, confidence[None], down, name="scale",
    )
    down_block, up_block = downs[own], ups[own]
    for k in range(1, half):
        earlier = [downs[ahead(k - 2)], ups[ahead(k - 2)]] if k >= 3 else []
        downs[behind(k)] = down_block = onward(after(down_block, *earlier))
        ups[behind(k)] = up_block = onward(up_block)
        downs[ahead(k)] = swap(down_block)
        ups[ahead(k)] = swap(up_block)
    earlier = [downs[ahead(half - 2)], ups[ahead(half - 2)]]
    mine = onward(after(pick(down_block, up_block), *earlier))
    near = [j for j in range(n) if j != opposite]
    preact = with_meta(
        functools.partial(preact_kernel, near), rank_f32, scaled, *(downs[j] for j in near),
        flops=2 * tokens * width * rank, name="preact",
    )
    mine = after(mine, preact)
    other = swap(mine)
    downs[opposite], ups[opposite] = pick(mine, other), pick(other, mine)

    pre_grad, mean, hidden_t, slope, preact, own_sum, *tops = with_meta(
        functools.partial(top_kernel, groups, opposite),
        [rank_bf16, shape(F32, tokens, 1), shape(BF16, rank, tokens), rank_f32, rank_f32, rank_f32]
        + [shape(BF16, len(slots), tokens, block) for slots in groups],
        x, teacher_states, scaled, weight_rows, preact, downs[opposite], *(ups[j] for j in range(n)),
        flops=4 * tokens * width * rank, name="top",
    )

    def leave(slots, cot, pre_grad, mean):
        return with_meta(
            functools.partial(leave_kernel, slots), shape(BF16, len(slots), tokens, block),
            cot, x, gains, pre_grad, inverse, mean, *(downs[j] for j in slots),
            flops=2 * len(slots) * tokens * block * rank, name="leave",
        )

    def arrive(i, value, total):
        slots, kind = groups[i], shape(BF16, *value.shape)
        body = functools.partial(arrive_kernel, total is not None, width, opposite)
        more, outs = [], [kind, rank_f32]
        if total is not None:
            more = [total, slope, preact, scaled]
            outs = [kind, rank_bf16, shape(BF16, rank, tokens), shape(F32, tokens, 1), half_part, half_part]
        outs = with_meta(
            body, outs + [part_shape] * len(slots), value, tops[i], hidden_t, *(ups[j] for j in slots), *more,
            flops=4 * len(slots) * tokens * block * rank, name="arrive",
        )
        return outs[: -len(slots)], outs[-len(slots) :]


    def split(total, part):
        return with_meta(
            split_kernel, [shape(F32, rank, half_block), shape(BF16, rank, half_block)],
            total, part, name="split",
        )

    cots = tops
    for hop in range(sections - 1):
        sent = [leave(slots, cot, pre_grad, mean) for slots, cot in zip(groups, cots)]
        arrived = [lax.ppermute(value, "section", back) for value in sent]
        if hop < sections - 2:
            (near_cot, hidden_grad), _ = arrive(0, arrived[0], None)
            (cot, pre_grad, _, mean, _, _), _ = arrive(1, arrived[1], hidden_grad)
            cots = [near_cot, cot]

    def finish(some, so_far):
        slots = [j for i in some for j in groups[i]]
        args = [x, gains, pre_grad, inverse, mean, *(downs[j] for j in slots), *(cots[i] for i in some)]
        given = [] if so_far is None else [so_far]
        return with_meta(
            functools.partial(finish_kernel, [groups[i] for i in some]), shape(BF16, tokens, width), *args, *given,
            specs=[VMEM] * len(args) + [ANY] * len(given), out_specs=[ANY],
            scratch=[pltpu.VMEM((len(slots), tokens, block), BF16), pltpu.SemaphoreType.DMA((len(slots),))],
            aliases={len(args) + 1: 0} if given else {},
            flops=2 * len(slots) * tokens * block * rank, name="finish",
        )

    (near_cot, hidden_grad), parts = arrive(0, after(arrived[0], sent[1]), None)
    up_total = onward(parts[0])
    up_total = onward(add(part_shape, up_total, parts[1], swap(parts[2])))
    (cot, pre_grad, pre_t, mean, *far), parts = arrive(1, after(arrived[1], up_total), hidden_grad)
    cots = [near_cot, cot]
    down_totals = [onward(value) for value in far]
    behinds = with_meta(
        functools.partial(stack_kernel, [behind(k) for k in range(1, half)]),
        shape(BF16, 2 * (half - 1), rank, half_block), scaled, pre_t, name="products",
    )
    swapped = swap(behinds)
    slots = [ahead(k) for k in range(1, half)] + [own]
    halves = with_meta(
        functools.partial(products_kernel, slots), [half_part] * (2 * len(slots)), scaled, pre_t, name="products"
    )
    input_grads = None
    for at, k in enumerate(range(half - 1, 0, -1)):
        if k < half - 1:
            i = 2 * (half - 2 - k)
            up_total = onward(add(part_shape, up_total, parts[i], swap(parts[i + 1])))
        down_totals = [
            onward(add(half_part, down_totals[c], halves[2 * (k - 1) + c], (swapped, 2 * (k - 1) + c))) for c in (0, 1)
        ]
        if at < len(groups):
            input_grads = finish([at], input_grads)
            down_totals[1] = after(down_totals[1], input_grads)
    up_mine, up_other = split(up_total, parts[-1])
    up_other = swap(up_other)
    grad_up = call(
        functools.partial(close_kernel, tokens), shape(F32, 1, half_block, rank), up_mine, up_other, name="close_up"
    )
    down_mine, down_other = with_meta(
        split_halves_kernel, [shape(F32, rank, half_block), half_part], *down_totals, *halves[-2:], name="split"
    )
    down_other = swap(down_other)
    grad_down, grad_gain = with_meta(
        functools.partial(close_gain_kernel, tokens),
        [shape(F32, 1, half_block, rank), shape(F32, 1, half_block)],
        down_mine, down_other, down_t, gains, name="close_down",
    )
    return input_grads[None], grad_down, grad_up, grad_gain


def solution(mesh):
    in_specs = (
        P("section", "dp", None),
        P("dp", None),
        P("dp"),
        P("section", None),
        P("section", "dp", None),
        P("section", "dp", None),
    )
    out_specs = (
        P("section", "dp", None),
        P("section", "dp", None),
        P("section", "dp", None),
        P("section", "dp"),
    )
    return jax.shard_map(local, mesh=mesh, in_specs=in_specs, out_specs=out_specs, check_vma=False)
```

```python
import functools

import jax
import jax.numpy as jnp
import numpy as np
from jax import lax
from jax.experimental import pallas as pl
from jax.experimental.pallas import tpu as pltpu
from jax.sharding import PartitionSpec as P

Z_CHIPS = 4
CORES = 2
EPSILON = 1e-05
F32 = jnp.float32
BF16 = jnp.bfloat16
VMEM = pl.BlockSpec(memory_space=pltpu.VMEM)
SMEM = pl.BlockSpec(memory_space=pltpu.SMEM)
ANY = pl.BlockSpec(memory_space=pl.ANY)
NT = (((1,), (1,)), ((), ()))


def ring_of_chips(chips):
    rows = chips // Z_CHIPS
    cycle = []
    for z in range(Z_CHIPS):
        ys = range(1, rows) if z % 2 == 0 else range(rows - 1, 0, -1)
        cycle += [z * rows + y for y in ys]
    return cycle + [z * rows for z in range(Z_CHIPS - 1, -1, -1)]


class Routes:
    def __init__(self, devices):
        ring = ring_of_chips(devices // CORES)
        n = self.n = len(ring)
        half = self.half = n // 2
        self.partner = [(i, i ^ 1) for i in range(devices)]
        self.onward = [
            (ring[i] * CORES + c, ring[(i + 1 - 2 * c) % n] * CORES + c) for c in range(CORES) for i in range(n)
        ]
        steps = [s for k in range(1, half) for s in (-k, k)] + [half, 0]
        self.table = np.zeros((devices, n), np.int32)
        for i, chip in enumerate(ring):
            for c in range(CORES):
                self.table[chip * CORES + c] = [ring[(i + (1 - 2 * c) * s) % n] for s in steps]
        self.opposite, self.own = n - 2, n - 1
        leaving = [self.opposite] + [f(k) for k in range(half - 1, 0, -1) for f in (self.ahead, self.behind)] + [self.own]
        self.groups = [leaving[:3], leaving[3:-3], leaving[-3:]]

    def behind(self, k):
        return 2 * k - 2

    def ahead(self, k):
        return 2 * k - 1


def after(value, *earlier):
    return lax.optimization_barrier((value, *earlier))[0] if earlier else value


def call(body, outs, *args, specs=None, out_specs=None, scratch=(), flops=0, aliases=None, vmem=8, name=None):
    single = not isinstance(outs, (list, tuple))
    outs = [outs] if single else list(outs)
    moved = sum(a.size * a.dtype.itemsize for a in args) + sum(o.size * o.dtype.itemsize for o in outs)
    result = pl.pallas_call(
        body,
        in_specs=specs or [VMEM] * len(args),
        out_specs=out_specs or [VMEM] * len(outs),
        out_shape=outs,
        scratch_shapes=scratch,
        input_output_aliases=aliases or {},
        cost_estimate=pl.CostEstimate(flops=flops, bytes_accessed=moved // 4, transcendentals=0),
        compiler_params=pltpu.CompilerParams(vmem_limit_bytes=vmem << 20),
        name=name,
    )(*args)
    return result[0] if single else result


class Place:
    def __init__(self, sections, table_ref):
        self.table, self.sections, self.n = table_ref, sections, table_ref.shape[1]

    def __getitem__(self, slot):
        return self.table[lax.axis_index("dp"), slot]

    def first(self):
        return lax.axis_index("dp") % CORES == 0

    def last(self):
        return lax.axis_index("section") == self.sections - 1


def placed(body, sections):
    def kernel(table_ref, *refs):
        body(Place(sections, table_ref), *refs)

    return kernel


def shape(dtype, *dims):
    return jax.ShapeDtypeStruct(dims, dtype)


def columns(ref, chip, block):
    return ref[:, pl.ds(pl.multiple_of(chip * block, block), block)]


def scale_kernel(block, x_ref, gain_ref, conf_ref, down_ref, inv_ref, scaled_ref, weight_ref, down_t_ref):
    tokens, width = x_ref.shape
    squares = jnp.zeros((tokens, block), F32)
    for at in range(0, width, block):
        values = x_ref[:, at : at + block].astype(F32)
        squares = squares + values * values
    inverse = lax.rsqrt(jnp.sum(squares, axis=-1, keepdims=True) / width + EPSILON)
    inv_ref[...] = inverse
    for at in range(0, width, block):
        values = x_ref[:, at : at + block].astype(F32)
        scaled_ref[:, at : at + block] = ((values * inverse) * gain_ref[:, at : at + block]).astype(BF16)
    weights = jnp.broadcast_to(conf_ref[...].astype(F32) / 256.0, (tokens, tokens))
    row = lax.broadcasted_iota(jnp.int32, (tokens, tokens), 0)
    column = lax.broadcasted_iota(jnp.int32, (tokens, tokens), 1)
    weight_ref[...] = jnp.sum(jnp.where(row == column, weights, 0.0), axis=1, keepdims=True)
    down_t_ref[...] = down_ref[...].astype(F32).T


def assemble_kernel(mine_ref, other_ref, out_ref, sems):
    rows = mine_ref.shape[0]
    core = lax.axis_index("dp") % CORES
    copies = []
    for i, (ref, place) in enumerate(((mine_ref, core), (other_ref, 1 - core))):
        out = out_ref.at[pl.ds(pl.multiple_of(place * rows, rows), rows)]
        copies.append(pltpu.make_async_copy(ref, out, sems.at[i]))
        copies[-1].start()
    for copy in copies:
        copy.wait()


def pick_kernel(zero_ref, one_ref, out_ref, sem):
    core = lax.axis_index("dp") % CORES
    for at, ref in enumerate((zero_ref, one_ref)):

        @pl.when(core == at)
        def _():
            copy = pltpu.make_async_copy(ref, out_ref, sem)
            copy.start()
            copy.wait()


def pre_grad_of(hidden_grad, slope, preact, width):
    pre_grad = (hidden_grad * slope).astype(BF16)
    return pre_grad, jnp.sum(pre_grad.astype(F32) * preact, axis=-1, keepdims=True) / width


def preact_kernel(slots, meta, scaled_ref, *refs):
    downs, out_ref = refs[:-1], refs[-1]
    total = 0.0
    for slot, down_ref in zip(slots, downs):
        scaled = columns(scaled_ref, meta[slot], down_ref.shape[0])
        total = total + jnp.dot(scaled, down_ref[...], preferred_element_type=F32)
    out_ref[...] = total


def top_kernel(groups, opposite, meta, x_ref, t_ref, scaled_ref, weight_ref, sum_ref, down_ref, *refs):
    n = meta.n
    ups, (pre_out, mean_out, hid_out, slope_out, preact_out, sum_out, *tops) = refs[:n], refs[n:]
    width = x_ref.shape[1]
    block = width // n
    far = columns(scaled_ref, meta[opposite], block)
    preact = sum_ref[...] + jnp.dot(far, down_ref[...], preferred_element_type=F32)
    sigmoid_val = 1.0 / (1.0 + jnp.exp(-preact))
    slope = sigmoid_val * (1.0 + preact * (1.0 - sigmoid_val))
    hidden = preact * sigmoid_val
    preact_out[...] = preact
    slope_out[...] = slope
    hid_out[...] = hidden.T.astype(BF16)
    hidden = hidden.astype(BF16)
    weight = weight_ref[...]
    total = jnp.zeros_like(preact)
    for group, top_ref in zip(groups, tops):
        for at, slot in enumerate(group):
            branch = lax.dot_general(hidden, ups[slot][...], NT, preferred_element_type=F32)
            chip = meta[slot]
            values = columns(x_ref, chip, block).astype(F32) + branch - columns(t_ref, chip, block).astype(F32)
            top = (weight * values).astype(BF16)
            top_ref[at] = top
            total = total + jnp.dot(top, ups[slot][...], preferred_element_type=F32)
    sum_out[...] = total
    pre_out[...], mean_out[...] = pre_grad_of(total, slope, preact, width)


def input_grad(cot, x, down, gain, pre_grad, inverse, mean):
    grad = lax.dot_general(pre_grad, down, NT, preferred_element_type=F32)
    return (cot.astype(F32) + inverse * (grad * gain - x.astype(F32) * inverse * mean)).astype(BF16)


def leave_kernel(slots, meta, cot_ref, x_ref, gain_ref, pre_ref, inv_ref, mean_ref, *refs):
    downs, out_ref = refs[:-1], refs[-1]
    for at, slot in enumerate(slots):
        block = downs[at].shape[0]
        x, gain = columns(x_ref, meta[slot], block), columns(gain_ref, meta[slot], block)
        out_ref[at] = input_grad(cot_ref[at], x, downs[at][...], gain, pre_ref[...], inv_ref[...], mean_ref[...])


def arrive_kernel(follows, ends, width, opposite, meta, arrived_ref, top_ref, hid_ref, *refs):
    count = arrived_ref.shape[0]
    ups, refs = refs[:count], refs[count:]
    total = 0.0
    if follows:
        total = refs[0][...]
        refs = refs[1:]
    if ends:
        slope_ref, preact_ref, scaled_ref, cot_ref, pre_out, pre_t_out, mean_out, *outs = refs
        outs, parts = outs[:2], outs[2:]
    else:
        cot_ref, sum_out, *parts = refs
    for at in range(count):
        cot = jnp.where(meta.last(), top_ref[at], arrived_ref[at])
        cot_ref[at] = cot
        total = total + jnp.dot(cot, ups[at][...], preferred_element_type=F32)
        parts[at][...] = jnp.dot(hid_ref[...], cot, preferred_element_type=F32).astype(BF16)
    if not ends:
        sum_out[...] = total
        return
    pre_out[...], mean_out[...] = pre_grad_of(total, slope_ref[...], preact_ref[...], width)
    pre_t = (total * slope_ref[...]).T.astype(BF16)
    pre_t_out[...] = pre_t
    put_product(pre_t, columns(scaled_ref, meta[opposite], ups[0].shape[0]), outs)


def put_product(pre_t, scaled, halves):
    part = jnp.dot(pre_t, scaled, preferred_element_type=F32).astype(BF16)
    half = part.shape[1] // 2
    halves[0][...] = part[:, :half]
    halves[1][...] = part[:, half:]


def products_kernel(slots, meta, scaled_ref, pre_t_ref, *outs):
    for at, slot in enumerate(slots):
        halves = outs[2 * at : 2 * at + 2]
        put_product(pre_t_ref[...], columns(scaled_ref, meta[slot], 2 * halves[0].shape[1]), halves)


def stack_kernel(slots, meta, scaled_ref, pre_t_ref, out_ref):
    for at, slot in enumerate(slots):
        halves = out_ref.at[2 * at], out_ref.at[2 * at + 1]
        put_product(pre_t_ref[...], columns(scaled_ref, meta[slot], 2 * out_ref.shape[2]), halves)


def add_kernel(picks, *refs):
    out_ref = refs[-1]
    total = None
    for ref, pick in zip(refs[:-1], picks):
        value = (ref[...] if pick is None else ref[pick]).astype(F32)
        total = value if total is None else total + value
    out_ref[...] = total.astype(out_ref.dtype)


def add(out, *terms):
    arrays = [t[0] if isinstance(t, tuple) else t for t in terms]
    picks = [t[1] if isinstance(t, tuple) else None for t in terms]
    return call(functools.partial(add_kernel, picks), out, *arrays, name="add")


def split_kernel(meta, total_ref, part_ref, mine_ref, other_ref):
    half = mine_ref.shape[1]
    first = meta.first()
    low = total_ref[:, :half].astype(F32) + part_ref[:, :half].astype(F32)
    high = total_ref[:, half:].astype(F32) + part_ref[:, half:].astype(F32)
    mine_ref[...] = jnp.where(first, low, high)
    other_ref[...] = jnp.where(first, high, low).astype(BF16)


def split_halves_kernel(meta, low_ref, high_ref, low_part, high_part, mine_ref, other_ref):
    first = meta.first()
    low = low_ref[...].astype(F32) + low_part[...].astype(F32)
    high = high_ref[...].astype(F32) + high_part[...].astype(F32)
    mine_ref[...] = jnp.where(first, low, high)
    other_ref[...] = jnp.where(first, high, low).astype(BF16)


def close_kernel(tokens, mine_ref, other_ref, grad_ref):
    grad_ref[0] = ((mine_ref[...] + other_ref[...].astype(F32)) / tokens).T


def close_gain_kernel(tokens, meta, mine_ref, other_ref, down_t_ref, gain_ref, grad_ref, gain_grad_ref):
    grad = (mine_ref[...] + other_ref[...].astype(F32)) / tokens
    grad_ref[0] = grad.T
    columns_own = grad.shape[1]
    gain = columns(gain_ref, lax.axis_index("dp"), columns_own)
    gain_grad_ref[...] = jnp.sum(grad * down_t_ref[...], axis=0, keepdims=True) / gain


def finish_kernel(groups, meta, x_ref, gain_ref, pre_ref, inv_ref, mean_ref, *refs):
    slots = [slot for group in groups for slot in group]
    downs, cots = refs[: len(slots)], refs[len(slots) : len(slots) + len(groups)]
    out_ref, held, sems = refs[-3:]
    copies = []
    for group, cot_ref in zip(groups, cots):
        for at, slot in enumerate(group):
            i = len(copies)
            down = downs[i][...]
            block = down.shape[0]
            chip = meta[slot]
            x, gain = columns(x_ref, chip, block), columns(gain_ref, chip, block)
            held[i] = input_grad(cot_ref[at], x, down, gain, pre_ref[...], inv_ref[...], mean_ref[...])
            place = out_ref.at[:, pl.ds(pl.multiple_of(chip * block, block), block)]
            copies.append(pltpu.make_async_copy(held.at[i], place, sems.at[i]))
            copies[-1].start()
    for copy in copies:
        copy.wait()


def local(section_inputs, teacher_states, confidence, gains, w_down, w_up):
    sections = lax.axis_size("section")
    devices = lax.axis_size("dp")
    routes = Routes(devices)
    n, half, opposite, own, groups = routes.n, routes.half, routes.opposite, routes.own, routes.groups
    behind, ahead = routes.behind, routes.ahead
    x = section_inputs[0]
    tokens, width = x.shape
    block = width // n
    rank = w_down.shape[2]
    half_block = block // CORES
    back = [(s, s - 1) for s in range(1, sections)]

    def swap(value):
        return lax.ppermute(value, "dp", routes.partner)

    def onward(value):
        return lax.ppermute(value, "dp", routes.onward)

    rank_f32, rank_bf16 = shape(F32, tokens, rank), shape(BF16, tokens, rank)
    half_part = shape(BF16, rank, block // CORES)
    chunk, part_shape = shape(BF16, block, rank), shape(BF16, rank, block)

    def of_chip(mine, other):
        return call(
            assemble_kernel, chunk, mine, other, specs=[ANY] * 2, scratch=[pltpu.SemaphoreType.DMA((2,))], name="assemble"
        )

    def pick(zero, one):
        return call(pick_kernel, chunk, zero, one, specs=[ANY] * 2, scratch=[pltpu.SemaphoreType.DMA], name="pick")

    down, up = w_down[0], w_up[0]
    downs, ups = {}, {}
    downs[own] = of_chip(down, swap(down))
    ups[own] = of_chip(up, swap(up))
    table = jnp.asarray(routes.table)

    def with_meta(body, outs, *args, **kw):
        specs = [SMEM] + kw.pop("specs", [VMEM] * len(args))
        return call(placed(body, sections), outs, table, *args, specs=specs, **kw)

    inverse, scaled, weight_rows, down_t = call(
        functools.partial(scale_kernel, block),
        [shape(F32, tokens, 1), shape(BF16, tokens, width), shape(F32, tokens, 1), shape(F32, rank, half_block)],
        after(x, downs[own]), gains, confidence[None], down, name="scale",
    )
    down_block, up_block = downs[own], ups[own]
    for k in range(1, half):
        earlier = [downs[ahead(k - 2)], ups[ahead(k - 2)]] if k >= 3 else []
        downs[behind(k)] = down_block = onward(after(down_block, *earlier))
        ups[behind(k)] = up_block = onward(up_block)
        downs[ahead(k)] = swap(down_block)
        ups[ahead(k)] = swap(up_block)
    earlier = [downs[ahead(half - 2)], ups[ahead(half - 2)]]
    mine = onward(after(pick(down_block, up_block), *earlier))
    near = [j for j in range(n) if j != opposite]
    preact = with_meta(
        functools.partial(preact_kernel, near), rank_f32, scaled, *(downs[j] for j in near),
        flops=2 * tokens * width * rank, name="preact",
    )
    mine = after(mine, preact)
    other = swap(mine)
    downs[opposite], ups[opposite] = pick(mine, other), pick(other, mine)

    pre_grad, mean, hidden_t, slope, preact, own_sum, *tops = with_meta(
        functools.partial(top_kernel, groups, opposite),
        [rank_bf16, shape(F32, tokens, 1), shape(BF16, rank, tokens), rank_f32, rank_f32, rank_f32]
        + [shape(BF16, len(slots), tokens, block) for slots in groups],
        x, teacher_states, scaled, weight_rows, preact, downs[opposite], *(ups[j] for j in range(n)),
        flops=4 * tokens * width * rank, name="top",
    )

    def leave(slots, cot, pre_grad, mean):
        return with_meta(
            functools.partial(leave_kernel, slots), shape(BF16, len(slots), tokens, block),
            cot, x, gains, pre_grad, inverse, mean, *(downs[j] for j in slots),
            flops=2 * len(slots) * tokens * block * rank, name="leave",
        )

    def arrive(i, value, total):
        slots, kind = groups[i], shape(BF16, *value.shape)
        ends = i == len(groups) - 1
        body = functools.partial(arrive_kernel, total is not None, ends, width, opposite)
        more, outs = [] if total is None else [total], [kind, rank_f32]
        if ends:
            more += [slope, preact, scaled]
            outs = [kind, rank_bf16, shape(BF16, rank, tokens), shape(F32, tokens, 1), half_part, half_part]
        outs = with_meta(
            body, outs + [part_shape] * len(slots), value, tops[i], hidden_t, *(ups[j] for j in slots), *more,
            flops=4 * len(slots) * tokens * block * rank, name="arrive",
        )
        return outs[: -len(slots)], outs[-len(slots) :]


    def split(total, part):
        return with_meta(
            split_kernel, [shape(F32, rank, half_block), shape(BF16, rank, half_block)],
            total, part, name="split",
        )

    cots = tops
    for hop in range(sections - 1):
        sent = [leave(slots, cot, pre_grad, mean) for slots, cot in zip(groups, cots)]
        arrived = [lax.ppermute(value, "section", back) for value in sent]
        if hop < sections - 2:
            (first_cot, hidden_grad), _ = arrive(0, arrived[0], None)
            (second_cot, hidden_grad), _ = arrive(1, arrived[1], hidden_grad)
            (third_cot, pre_grad, _, mean, _, _), _ = arrive(2, arrived[2], hidden_grad)
            cots = [first_cot, second_cot, third_cot]

    def finish(some, so_far):
        slots = [j for i in some for j in groups[i]]
        args = [x, gains, pre_grad, inverse, mean, *(downs[j] for j in slots), *(cots[i] for i in some)]
        given = [] if so_far is None else [so_far]
        return with_meta(
            functools.partial(finish_kernel, [groups[i] for i in some]), shape(BF16, tokens, width), *args, *given,
            specs=[VMEM] * len(args) + [ANY] * len(given), out_specs=[ANY],
            scratch=[pltpu.VMEM((len(slots), tokens, block), BF16), pltpu.SemaphoreType.DMA((len(slots),))],
            aliases={len(args) + 1: 0} if given else {},
            flops=2 * len(slots) * tokens * block * rank, name="finish",
        )

    def step(total, part, other):
        return add(part_shape, total, part, swap(other))

    (first_cot, hidden_grad), parts = arrive(0, after(arrived[0], *sent[1:]), None)
    up_total = onward(parts[0])
    (second_cot, hidden_grad), more_parts = arrive(1, after(arrived[1], up_total), hidden_grad)
    up_sent = step(up_total, parts[1], parts[2])
    for at in range(0, len(more_parts), 2):
        up_sent = step(onward(up_sent), more_parts[at], more_parts[at + 1])
    (third_cot, pre_grad, pre_t, mean, *far), parts = arrive(2, after(arrived[2], up_sent), hidden_grad)
    cots = [first_cot, second_cot, third_cot]
    up_total = onward(step(onward(up_sent), parts[0], parts[1]))
    down_totals = [onward(value) for value in far]
    behinds = with_meta(
        functools.partial(stack_kernel, [behind(k) for k in range(1, half)]),
        shape(BF16, 2 * (half - 1), rank, half_block), scaled, pre_t, name="products",
    )
    swapped = swap(behinds)
    slots = [ahead(k) for k in range(1, half)] + [own]
    halves = with_meta(
        functools.partial(products_kernel, slots), [half_part] * (2 * len(slots)), scaled, pre_t, name="products"
    )
    input_grads = None
    for at, k in enumerate(range(half - 1, 0, -1)):
        down_totals = [
            onward(add(half_part, down_totals[c], halves[2 * (k - 1) + c], (swapped, 2 * (k - 1) + c))) for c in (0, 1)
        ]
        if at == 0:
            input_grads = finish([0, 1], None)
            down_totals[1] = after(down_totals[1], input_grads)
    input_grads = finish([2], input_grads)
    down_totals[1] = after(down_totals[1], input_grads)
    up_mine, up_other = split(up_total, parts[-1])
    up_other = swap(up_other)
    grad_up = call(
        functools.partial(close_kernel, tokens), shape(F32, 1, half_block, rank), up_mine, up_other, name="close_up"
    )
    down_mine, down_other = with_meta(
        split_halves_kernel, [shape(F32, rank, half_block), half_part], *down_totals, *halves[-2:], name="split"
    )
    down_other = swap(down_other)
    grad_down, grad_gain = with_meta(
        functools.partial(close_gain_kernel, tokens),
        [shape(F32, 1, half_block, rank), shape(F32, 1, half_block)],
        down_mine, down_other, down_t, gains, name="close_down",
    )
    return input_grads[None], grad_down, grad_up, grad_gain


def solution(mesh):
    in_specs = (
        P("section", "dp", None),
        P("dp", None),
        P("dp"),
        P("section", None),
        P("section", "dp", None),
        P("section", "dp", None),
    )
    out_specs = (
        P("section", "dp", None),
        P("section", "dp", None),
        P("section", "dp", None),
        P("section", "dp"),
    )
    return jax.shard_map(local, mesh=mesh, in_specs=in_specs, out_specs=out_specs, check_vma=False)
```

```python
import functools

import jax
import jax.numpy as jnp
import numpy as np
from jax import lax
from jax.experimental import pallas as pl
from jax.experimental.pallas import tpu as pltpu
from jax.sharding import PartitionSpec as P

Z_CHIPS = 4
CORES = 2
EPSILON = 1e-05
F32 = jnp.float32
BF16 = jnp.bfloat16
VMEM = pl.BlockSpec(memory_space=pltpu.VMEM)
SMEM = pl.BlockSpec(memory_space=pltpu.SMEM)
ANY = pl.BlockSpec(memory_space=pl.ANY)
NT = (((1,), (1,)), ((), ()))


def ring_of_chips(chips):
    rows = chips // Z_CHIPS
    cycle = []
    for z in range(Z_CHIPS):
        ys = range(1, rows) if z % 2 == 0 else range(rows - 1, 0, -1)
        cycle += [z * rows + y for y in ys]
    return cycle + [z * rows for z in range(Z_CHIPS - 1, -1, -1)]


class Routes:
    def __init__(self, devices):
        ring = ring_of_chips(devices // CORES)
        n = self.n = len(ring)
        half = self.half = n // 2
        self.partner = [(i, i ^ 1) for i in range(devices)]
        self.onward = [
            (ring[i] * CORES + c, ring[(i + 1 - 2 * c) % n] * CORES + c) for c in range(CORES) for i in range(n)
        ]
        steps = [s for k in range(1, half) for s in (-k, k)] + [half, 0]
        self.table = np.zeros((devices, n), np.int32)
        for i, chip in enumerate(ring):
            for c in range(CORES):
                self.table[chip * CORES + c] = [ring[(i + (1 - 2 * c) * s) % n] for s in steps]
        self.opposite, self.own = n - 2, n - 1
        leaving = [self.opposite] + [f(k) for k in range(half - 1, 0, -1) for f in (self.ahead, self.behind)] + [self.own]
        self.groups = [leaving[:3], leaving[3:-3], leaving[-3:]]

    def behind(self, k):
        return 2 * k - 2

    def ahead(self, k):
        return 2 * k - 1


def after(value, *earlier):
    return lax.optimization_barrier((value, *earlier))[0] if earlier else value


def call(body, outs, *args, specs=None, out_specs=None, scratch=(), flops=0, aliases=None, vmem=8, name=None):
    single = not isinstance(outs, (list, tuple))
    outs = [outs] if single else list(outs)
    moved = sum(a.size * a.dtype.itemsize for a in args) + sum(o.size * o.dtype.itemsize for o in outs)
    result = pl.pallas_call(
        body,
        in_specs=specs or [VMEM] * len(args),
        out_specs=out_specs or [VMEM] * len(outs),
        out_shape=outs,
        scratch_shapes=scratch,
        input_output_aliases=aliases or {},
        cost_estimate=pl.CostEstimate(flops=flops, bytes_accessed=moved // 4, transcendentals=0),
        compiler_params=pltpu.CompilerParams(vmem_limit_bytes=vmem << 20),
        name=name,
    )(*args)
    return result[0] if single else result


class Place:
    def __init__(self, sections, table_ref):
        self.table, self.sections, self.n = table_ref, sections, table_ref.shape[1]

    def __getitem__(self, slot):
        return self.table[lax.axis_index("dp"), slot]

    def first(self):
        return lax.axis_index("dp") % CORES == 0

    def last(self):
        return lax.axis_index("section") == self.sections - 1


def placed(body, sections):
    def kernel(table_ref, *refs):
        body(Place(sections, table_ref), *refs)

    return kernel


def shape(dtype, *dims):
    return jax.ShapeDtypeStruct(dims, dtype)


def columns(ref, chip, block):
    return ref[:, pl.ds(pl.multiple_of(chip * block, block), block)]


def scale_kernel(block, x_ref, gain_ref, conf_ref, down_ref, inv_ref, scaled_ref, weight_ref, down_t_ref):
    tokens, width = x_ref.shape
    squares = jnp.zeros((tokens, block), F32)
    for at in range(0, width, block):
        values = x_ref[:, at : at + block].astype(F32)
        squares = squares + values * values
    inverse = lax.rsqrt(jnp.sum(squares, axis=-1, keepdims=True) / width + EPSILON)
    inv_ref[...] = inverse
    for at in range(0, width, block):
        values = x_ref[:, at : at + block].astype(F32)
        scaled_ref[:, at : at + block] = ((values * inverse) * gain_ref[:, at : at + block]).astype(BF16)
    weights = jnp.broadcast_to(conf_ref[...].astype(F32) / 256.0, (tokens, tokens))
    row = lax.broadcasted_iota(jnp.int32, (tokens, tokens), 0)
    column = lax.broadcasted_iota(jnp.int32, (tokens, tokens), 1)
    weight_ref[...] = jnp.sum(jnp.where(row == column, weights, 0.0), axis=1, keepdims=True)
    down_t_ref[...] = down_ref[...].astype(F32).T


def assemble_kernel(mine_ref, other_ref, out_ref, sems):
    rows = mine_ref.shape[0]
    core = lax.axis_index("dp") % CORES
    copies = []
    for i, (ref, place) in enumerate(((mine_ref, core), (other_ref, 1 - core))):
        out = out_ref.at[pl.ds(pl.multiple_of(place * rows, rows), rows)]
        copies.append(pltpu.make_async_copy(ref, out, sems.at[i]))
        copies[-1].start()
    for copy in copies:
        copy.wait()


def pick_kernel(zero_ref, one_ref, out_ref, sem):
    core = lax.axis_index("dp") % CORES
    for at, ref in enumerate((zero_ref, one_ref)):

        @pl.when(core == at)
        def _():
            copy = pltpu.make_async_copy(ref, out_ref, sem)
            copy.start()
            copy.wait()


def pre_grad_of(hidden_grad, slope, preact, width):
    pre_grad = (hidden_grad * slope).astype(BF16)
    return pre_grad, jnp.sum(pre_grad.astype(F32) * preact, axis=-1, keepdims=True) / width


def preact_kernel(slots, meta, scaled_ref, *refs):
    downs, out_ref = refs[:-1], refs[-1]
    total = 0.0
    for slot, down_ref in zip(slots, downs):
        scaled = columns(scaled_ref, meta[slot], down_ref.shape[0])
        total = total + jnp.dot(scaled, down_ref[...], preferred_element_type=F32)
    out_ref[...] = total


def top_kernel(groups, opposite, meta, x_ref, t_ref, scaled_ref, weight_ref, sum_ref, down_ref, *refs):
    n = meta.n
    ups, (pre_out, mean_out, hid_out, slope_out, preact_out, sum_out, *tops) = refs[:n], refs[n:]
    width = x_ref.shape[1]
    block = width // n
    far = columns(scaled_ref, meta[opposite], block)
    preact = sum_ref[...] + jnp.dot(far, down_ref[...], preferred_element_type=F32)
    sigmoid_val = 1.0 / (1.0 + jnp.exp(-preact))
    slope = sigmoid_val * (1.0 + preact * (1.0 - sigmoid_val))
    hidden = preact * sigmoid_val
    preact_out[...] = preact
    slope_out[...] = slope
    hid_out[...] = hidden.T.astype(BF16)
    hidden = hidden.astype(BF16)
    weight = weight_ref[...]
    total = jnp.zeros_like(preact)
    for group, top_ref in zip(groups, tops):
        for at, slot in enumerate(group):
            branch = lax.dot_general(hidden, ups[slot][...], NT, preferred_element_type=F32)
            chip = meta[slot]
            values = columns(x_ref, chip, block).astype(F32) + branch - columns(t_ref, chip, block).astype(F32)
            top = (weight * values).astype(BF16)
            top_ref[at] = top
            total = total + jnp.dot(top, ups[slot][...], preferred_element_type=F32)
    sum_out[...] = total
    pre_out[...], mean_out[...] = pre_grad_of(total, slope, preact, width)


def input_grad(cot, x, down, gain, pre_grad, inverse, mean):
    grad = lax.dot_general(pre_grad, down, NT, preferred_element_type=F32)
    return (cot.astype(F32) + inverse * (grad * gain - x.astype(F32) * inverse * mean)).astype(BF16)


def leave_kernel(slots, meta, cot_ref, x_ref, gain_ref, pre_ref, inv_ref, mean_ref, *refs):
    downs, out_ref = refs[:-1], refs[-1]
    for at, slot in enumerate(slots):
        block = downs[at].shape[0]
        x, gain = columns(x_ref, meta[slot], block), columns(gain_ref, meta[slot], block)
        out_ref[at] = input_grad(cot_ref[at], x, downs[at][...], gain, pre_ref[...], inv_ref[...], mean_ref[...])


def arrive_kernel(follows, ends, width, opposite, meta, arrived_ref, top_ref, hid_ref, *refs):
    count = arrived_ref.shape[0]
    ups, refs = refs[:count], refs[count:]
    total = 0.0
    if follows:
        total = refs[0][...]
        refs = refs[1:]
    if ends:
        slope_ref, preact_ref, scaled_ref, cot_ref, pre_out, pre_t_out, mean_out, *outs = refs
        outs, parts = outs[:2], outs[2:]
    else:
        cot_ref, sum_out, *parts = refs
    for at in range(count):
        cot = jnp.where(meta.last(), top_ref[at], arrived_ref[at])
        cot_ref[at] = cot
        total = total + jnp.dot(cot, ups[at][...], preferred_element_type=F32)
        parts[at][...] = jnp.dot(hid_ref[...], cot, preferred_element_type=F32).astype(BF16)
    if not ends:
        sum_out[...] = total
        return
    pre_out[...], mean_out[...] = pre_grad_of(total, slope_ref[...], preact_ref[...], width)
    pre_t = (total * slope_ref[...]).T.astype(BF16)
    pre_t_out[...] = pre_t
    put_product(pre_t, columns(scaled_ref, meta[opposite], ups[0].shape[0]), outs)


def put_product(pre_t, scaled, halves):
    part = jnp.dot(pre_t, scaled, preferred_element_type=F32).astype(BF16)
    half = part.shape[1] // 2
    halves[0][...] = part[:, :half]
    halves[1][...] = part[:, half:]


def products_kernel(slots, meta, scaled_ref, pre_t_ref, *outs):
    for at, slot in enumerate(slots):
        halves = outs[2 * at : 2 * at + 2]
        put_product(pre_t_ref[...], columns(scaled_ref, meta[slot], 2 * halves[0].shape[1]), halves)


def stack_kernel(slots, meta, scaled_ref, pre_t_ref, out_ref):
    for at, slot in enumerate(slots):
        halves = out_ref.at[2 * at], out_ref.at[2 * at + 1]
        put_product(pre_t_ref[...], columns(scaled_ref, meta[slot], 2 * out_ref.shape[2]), halves)


def add_kernel(picks, *refs):
    out_ref = refs[-1]
    total = None
    for ref, pick in zip(refs[:-1], picks):
        value = (ref[...] if pick is None else ref[pick]).astype(F32)
        total = value if total is None else total + value
    out_ref[...] = total.astype(out_ref.dtype)


def add(out, *terms):
    arrays = [t[0] if isinstance(t, tuple) else t for t in terms]
    picks = [t[1] if isinstance(t, tuple) else None for t in terms]
    return call(functools.partial(add_kernel, picks), out, *arrays, name="add")


def split_kernel(meta, total_ref, part_ref, mine_ref, other_ref):
    half = mine_ref.shape[1]
    first = meta.first()
    low = total_ref[:, :half].astype(F32) + part_ref[:, :half].astype(F32)
    high = total_ref[:, half:].astype(F32) + part_ref[:, half:].astype(F32)
    mine_ref[...] = jnp.where(first, low, high)
    other_ref[...] = jnp.where(first, high, low).astype(BF16)


def split_halves_kernel(meta, low_ref, high_ref, low_part, high_part, mine_ref, other_ref):
    first = meta.first()
    low = low_ref[...].astype(F32) + low_part[...].astype(F32)
    high = high_ref[...].astype(F32) + high_part[...].astype(F32)
    mine_ref[...] = jnp.where(first, low, high)
    other_ref[...] = jnp.where(first, high, low).astype(BF16)


def close_kernel(tokens, mine_ref, other_ref, grad_ref):
    grad_ref[0] = ((mine_ref[...] + other_ref[...].astype(F32)) / tokens).T


def close_gain_kernel(tokens, meta, mine_ref, other_ref, down_t_ref, gain_ref, grad_ref, gain_grad_ref):
    grad = (mine_ref[...] + other_ref[...].astype(F32)) / tokens
    grad_ref[0] = grad.T
    columns_own = grad.shape[1]
    gain = columns(gain_ref, lax.axis_index("dp"), columns_own)
    gain_grad_ref[...] = jnp.sum(grad * down_t_ref[...], axis=0, keepdims=True) / gain


def finish_kernel(groups, meta, x_ref, gain_ref, pre_ref, inv_ref, mean_ref, *refs):
    slots = [slot for group in groups for slot in group]
    downs, cots = refs[: len(slots)], refs[len(slots) : len(slots) + len(groups)]
    out_ref, held, sems = refs[-3:]
    copies = []
    for group, cot_ref in zip(groups, cots):
        for at, slot in enumerate(group):
            i = len(copies)
            down = downs[i][...]
            block = down.shape[0]
            chip = meta[slot]
            x, gain = columns(x_ref, chip, block), columns(gain_ref, chip, block)
            held[i] = input_grad(cot_ref[at], x, down, gain, pre_ref[...], inv_ref[...], mean_ref[...])
            place = out_ref.at[:, pl.ds(pl.multiple_of(chip * block, block), block)]
            copies.append(pltpu.make_async_copy(held.at[i], place, sems.at[i]))
            copies[-1].start()
    for copy in copies:
        copy.wait()


def local(section_inputs, teacher_states, confidence, gains, w_down, w_up):
    sections = lax.axis_size("section")
    devices = lax.axis_size("dp")
    routes = Routes(devices)
    n, half, opposite, own, groups = routes.n, routes.half, routes.opposite, routes.own, routes.groups
    behind, ahead = routes.behind, routes.ahead
    x = section_inputs[0]
    tokens, width = x.shape
    block = width // n
    rank = w_down.shape[2]
    half_block = block // CORES
    back = [(s, s - 1) for s in range(1, sections)]

    def swap(value):
        return lax.ppermute(value, "dp", routes.partner)

    def onward(value):
        return lax.ppermute(value, "dp", routes.onward)

    rank_f32, rank_bf16 = shape(F32, tokens, rank), shape(BF16, tokens, rank)
    half_part = shape(BF16, rank, block // CORES)
    chunk, part_shape = shape(BF16, block, rank), shape(BF16, rank, block)

    def of_chip(mine, other):
        return call(
            assemble_kernel, chunk, mine, other, specs=[ANY] * 2, scratch=[pltpu.SemaphoreType.DMA((2,))], name="assemble"
        )

    def pick(zero, one):
        return call(pick_kernel, chunk, zero, one, specs=[ANY] * 2, scratch=[pltpu.SemaphoreType.DMA], name="pick")

    down, up = w_down[0], w_up[0]
    downs, ups = {}, {}
    downs[own] = of_chip(down, swap(down))
    ups[own] = of_chip(up, swap(up))
    table = jnp.asarray(routes.table)

    def with_meta(body, outs, *args, **kw):
        specs = [SMEM] + kw.pop("specs", [VMEM] * len(args))
        return call(placed(body, sections), outs, table, *args, specs=specs, **kw)

    inverse, scaled, weight_rows, down_t = call(
        functools.partial(scale_kernel, block),
        [shape(F32, tokens, 1), shape(BF16, tokens, width), shape(F32, tokens, 1), shape(F32, rank, half_block)],
        after(x, downs[own]), gains, confidence[None], down, name="scale",
    )
    down_block, up_block = downs[own], ups[own]
    for k in range(1, half):
        earlier = []
        downs[behind(k)] = down_block = onward(after(down_block, *earlier))
        ups[behind(k)] = up_block = onward(up_block)
        downs[ahead(k)] = swap(down_block)
        ups[ahead(k)] = swap(up_block)
    earlier = [downs[ahead(half - 2)], ups[ahead(half - 2)]]
    mine = onward(after(pick(down_block, up_block), *earlier))
    near = [j for j in range(n) if j != opposite]
    preact = with_meta(
        functools.partial(preact_kernel, near), rank_f32, scaled, *(downs[j] for j in near),
        flops=2 * tokens * width * rank, name="preact",
    )
    mine = after(mine, preact)
    other = swap(mine)
    downs[opposite], ups[opposite] = pick(mine, other), pick(other, mine)

    pre_grad, mean, hidden_t, slope, preact, own_sum, *tops = with_meta(
        functools.partial(top_kernel, groups, opposite),
        [rank_bf16, shape(F32, tokens, 1), shape(BF16, rank, tokens), rank_f32, rank_f32, rank_f32]
        + [shape(BF16, len(slots), tokens, block) for slots in groups],
        x, teacher_states, scaled, weight_rows, preact, downs[opposite], *(ups[j] for j in range(n)),
        flops=4 * tokens * width * rank, name="top",
    )

    def leave(slots, cot, pre_grad, mean):
        return with_meta(
            functools.partial(leave_kernel, slots), shape(BF16, len(slots), tokens, block),
            cot, x, gains, pre_grad, inverse, mean, *(downs[j] for j in slots),
            flops=2 * len(slots) * tokens * block * rank, name="leave",
        )

    def arrive(i, value, total):
        slots, kind = groups[i], shape(BF16, *value.shape)
        ends = i == len(groups) - 1
        body = functools.partial(arrive_kernel, total is not None, ends, width, opposite)
        more, outs = [] if total is None else [total], [kind, rank_f32]
        if ends:
            more += [slope, preact, scaled]
            outs = [kind, rank_bf16, shape(BF16, rank, tokens), shape(F32, tokens, 1), half_part, half_part]
        outs = with_meta(
            body, outs + [part_shape] * len(slots), value, tops[i], hidden_t, *(ups[j] for j in slots), *more,
            flops=4 * len(slots) * tokens * block * rank, name="arrive",
        )
        return outs[: -len(slots)], outs[-len(slots) :]


    def split(total, part):
        return with_meta(
            split_kernel, [shape(F32, rank, half_block), shape(BF16, rank, half_block)],
            total, part, name="split",
        )

    cots = tops
    for hop in range(sections - 1):
        sent = [leave(slots, cot, pre_grad, mean) for slots, cot in zip(groups, cots)]
        arrived = [lax.ppermute(value, "section", back) for value in sent]
        if hop < sections - 2:
            (first_cot, hidden_grad), _ = arrive(0, arrived[0], None)
            (second_cot, hidden_grad), _ = arrive(1, arrived[1], hidden_grad)
            (third_cot, pre_grad, _, mean, _, _), _ = arrive(2, arrived[2], hidden_grad)
            cots = [first_cot, second_cot, third_cot]

    def finish(some, so_far):
        slots = [j for i in some for j in groups[i]]
        args = [x, gains, pre_grad, inverse, mean, *(downs[j] for j in slots), *(cots[i] for i in some)]
        given = [] if so_far is None else [so_far]
        return with_meta(
            functools.partial(finish_kernel, [groups[i] for i in some]), shape(BF16, tokens, width), *args, *given,
            specs=[VMEM] * len(args) + [ANY] * len(given), out_specs=[ANY],
            scratch=[pltpu.VMEM((len(slots), tokens, block), BF16), pltpu.SemaphoreType.DMA((len(slots),))],
            aliases={len(args) + 1: 0} if given else {},
            flops=2 * len(slots) * tokens * block * rank, name="finish",
        )

    def step(total, part, other):
        return add(part_shape, total, part, swap(other))

    (first_cot, hidden_grad), parts = arrive(0, after(arrived[0], *sent[1:]), None)
    up_total = onward(parts[0])
    (second_cot, hidden_grad), more_parts = arrive(1, after(arrived[1], up_total), hidden_grad)
    up_sent = step(up_total, parts[1], parts[2])
    for at in range(0, len(more_parts), 2):
        up_sent = step(onward(up_sent), more_parts[at], more_parts[at + 1])
    (third_cot, pre_grad, pre_t, mean, *far), parts = arrive(2, after(arrived[2], up_sent), hidden_grad)
    cots = [first_cot, second_cot, third_cot]
    up_total = onward(step(onward(up_sent), parts[0], parts[1]))
    down_totals = [onward(value) for value in far]
    behinds = with_meta(
        functools.partial(stack_kernel, [behind(k) for k in range(1, half)]),
        shape(BF16, 2 * (half - 1), rank, half_block), scaled, pre_t, name="products",
    )
    swapped = swap(behinds)
    slots = [ahead(k) for k in range(1, half)] + [own]
    halves = with_meta(
        functools.partial(products_kernel, slots), [half_part] * (2 * len(slots)), scaled, pre_t, name="products"
    )
    input_grads = None
    for at, k in enumerate(range(half - 1, 0, -1)):
        down_totals = [
            onward(add(half_part, down_totals[c], halves[2 * (k - 1) + c], (swapped, 2 * (k - 1) + c))) for c in (0, 1)
        ]
        if at == 0:
            input_grads = finish([0, 1], None)
            down_totals[1] = after(down_totals[1], input_grads)
    input_grads = finish([2], input_grads)
    down_totals[1] = after(down_totals[1], input_grads)
    up_mine, up_other = split(up_total, parts[-1])
    up_other = swap(up_other)
    grad_up = call(
        functools.partial(close_kernel, tokens), shape(F32, 1, half_block, rank), up_mine, up_other, name="close_up"
    )
    down_mine, down_other = with_meta(
        split_halves_kernel, [shape(F32, rank, half_block), half_part], *down_totals, *halves[-2:], name="split"
    )
    down_other = swap(down_other)
    grad_down, grad_gain = with_meta(
        functools.partial(close_gain_kernel, tokens),
        [shape(F32, 1, half_block, rank), shape(F32, 1, half_block)],
        down_mine, down_other, down_t, gains, name="close_down",
    )
    return input_grads[None], grad_down, grad_up, grad_gain


def solution(mesh):
    in_specs = (
        P("section", "dp", None),
        P("dp", None),
        P("dp"),
        P("section", None),
        P("section", "dp", None),
        P("section", "dp", None),
    )
    out_specs = (
        P("section", "dp", None),
        P("section", "dp", None),
        P("section", "dp", None),
        P("section", "dp"),
    )
    return jax.shard_map(local, mesh=mesh, in_specs=in_specs, out_specs=out_specs, check_vma=False)
```

```python
import functools

import jax
import jax.numpy as jnp
import numpy as np
from jax import lax
from jax.experimental import pallas as pl
from jax.experimental.pallas import tpu as pltpu
from jax.sharding import PartitionSpec as P

Z_CHIPS = 4
CORES = 2
EPSILON = 1e-05
F32 = jnp.float32
BF16 = jnp.bfloat16
VMEM = pl.BlockSpec(memory_space=pltpu.VMEM)
SMEM = pl.BlockSpec(memory_space=pltpu.SMEM)
ANY = pl.BlockSpec(memory_space=pl.ANY)
NT = (((1,), (1,)), ((), ()))


def ring_of_chips(chips):
    rows = chips // Z_CHIPS
    cycle = []
    for z in range(Z_CHIPS):
        ys = range(1, rows) if z % 2 == 0 else range(rows - 1, 0, -1)
        cycle += [z * rows + y for y in ys]
    return cycle + [z * rows for z in range(Z_CHIPS - 1, -1, -1)]


class Routes:
    def __init__(self, devices):
        ring = ring_of_chips(devices // CORES)
        n = self.n = len(ring)
        half = self.half = n // 2
        self.partner = [(i, i ^ 1) for i in range(devices)]
        self.onward = [
            (ring[i] * CORES + c, ring[(i + 1 - 2 * c) % n] * CORES + c) for c in range(CORES) for i in range(n)
        ]
        steps = [s for k in range(1, half) for s in (-k, k)] + [half, 0]
        self.table = np.zeros((devices, n), np.int32)
        for i, chip in enumerate(ring):
            for c in range(CORES):
                self.table[chip * CORES + c] = [ring[(i + (1 - 2 * c) * s) % n] for s in steps]
        self.opposite, self.own = n - 2, n - 1
        leaving = [self.opposite] + [f(k) for k in range(half - 1, 0, -1) for f in (self.ahead, self.behind)] + [self.own]
        self.groups = [leaving[:3], leaving[3:-3], leaving[-3:]]

    def behind(self, k):
        return 2 * k - 2

    def ahead(self, k):
        return 2 * k - 1


def after(value, *earlier):
    return lax.optimization_barrier((value, *earlier))[0] if earlier else value


def call(body, outs, *args, specs=None, out_specs=None, scratch=(), flops=0, aliases=None, vmem=8, name=None):
    single = not isinstance(outs, (list, tuple))
    outs = [outs] if single else list(outs)
    moved = sum(a.size * a.dtype.itemsize for a in args) + sum(o.size * o.dtype.itemsize for o in outs)
    result = pl.pallas_call(
        body,
        in_specs=specs or [VMEM] * len(args),
        out_specs=out_specs or [VMEM] * len(outs),
        out_shape=outs,
        scratch_shapes=scratch,
        input_output_aliases=aliases or {},
        cost_estimate=pl.CostEstimate(flops=flops, bytes_accessed=moved // 4, transcendentals=0),
        compiler_params=pltpu.CompilerParams(vmem_limit_bytes=vmem << 20),
        name=name,
    )(*args)
    return result[0] if single else result


class Place:
    def __init__(self, sections, table_ref):
        self.table, self.sections, self.n = table_ref, sections, table_ref.shape[1]

    def __getitem__(self, slot):
        return self.table[lax.axis_index("dp"), slot]

    def first(self):
        return lax.axis_index("dp") % CORES == 0

    def last(self):
        return lax.axis_index("section") == self.sections - 1


def placed(body, sections):
    def kernel(table_ref, *refs):
        body(Place(sections, table_ref), *refs)

    return kernel


def shape(dtype, *dims):
    return jax.ShapeDtypeStruct(dims, dtype)


def columns(ref, chip, block):
    return ref[:, pl.ds(pl.multiple_of(chip * block, block), block)]


def scale_kernel(block, x_ref, gain_ref, conf_ref, down_ref, inv_ref, scaled_ref, weight_ref, down_t_ref):
    tokens, width = x_ref.shape
    squares = jnp.zeros((tokens, block), F32)
    for at in range(0, width, block):
        values = x_ref[:, at : at + block].astype(F32)
        squares = squares + values * values
    inverse = lax.rsqrt(jnp.sum(squares, axis=-1, keepdims=True) / width + EPSILON)
    inv_ref[...] = inverse
    for at in range(0, width, block):
        values = x_ref[:, at : at + block].astype(F32)
        scaled_ref[:, at : at + block] = ((values * inverse) * gain_ref[:, at : at + block]).astype(BF16)
    weights = jnp.broadcast_to(conf_ref[...].astype(F32) / 256.0, (tokens, tokens))
    row = lax.broadcasted_iota(jnp.int32, (tokens, tokens), 0)
    column = lax.broadcasted_iota(jnp.int32, (tokens, tokens), 1)
    weight_ref[...] = jnp.sum(jnp.where(row == column, weights, 0.0), axis=1, keepdims=True)
    down_t_ref[...] = down_ref[...].astype(F32).T


def assemble_kernel(mine_ref, other_ref, out_ref, sems):
    rows = mine_ref.shape[0]
    core = lax.axis_index("dp") % CORES
    copies = []
    for i, (ref, place) in enumerate(((mine_ref, core), (other_ref, 1 - core))):
        out = out_ref.at[pl.ds(pl.multiple_of(place * rows, rows), rows)]
        copies.append(pltpu.make_async_copy(ref, out, sems.at[i]))
        copies[-1].start()
    for copy in copies:
        copy.wait()


def halve_kernel(block_ref, out_ref, sem):
    rows = out_ref.shape[0]
    core = lax.axis_index("dp") % CORES
    copy = pltpu.make_async_copy(block_ref.at[pl.ds(pl.multiple_of(core * rows, rows), rows)], out_ref, sem)
    copy.start()
    copy.wait()


def pre_grad_of(hidden_grad, slope, preact, width):
    pre_grad = (hidden_grad * slope).astype(BF16)
    return pre_grad, jnp.sum(pre_grad.astype(F32) * preact, axis=-1, keepdims=True) / width


def preact_kernel(slots, meta, scaled_ref, *refs):
    downs, out_ref = refs[:-1], refs[-1]
    total = 0.0
    for slot, down_ref in zip(slots, downs):
        scaled = columns(scaled_ref, meta[slot], down_ref.shape[0])
        total = total + jnp.dot(scaled, down_ref[...], preferred_element_type=F32)
    out_ref[...] = total


def top_kernel(groups, opposite, meta, x_ref, t_ref, scaled_ref, weight_ref, sum_ref, down_ref, *refs):
    n = meta.n
    ups, (pre_out, mean_out, hid_out, slope_out, preact_out, sum_out, *tops) = refs[:n], refs[n:]
    width = x_ref.shape[1]
    block = width // n
    far = columns(scaled_ref, meta[opposite], block)
    preact = sum_ref[...] + jnp.dot(far, down_ref[...], preferred_element_type=F32)
    sigmoid_val = 1.0 / (1.0 + jnp.exp(-preact))
    slope = sigmoid_val * (1.0 + preact * (1.0 - sigmoid_val))
    hidden = preact * sigmoid_val
    preact_out[...] = preact
    slope_out[...] = slope
    hid_out[...] = hidden.T.astype(BF16)
    hidden = hidden.astype(BF16)
    weight = weight_ref[...]
    total = jnp.zeros_like(preact)
    for group, top_ref in zip(groups, tops):
        for at, slot in enumerate(group):
            branch = lax.dot_general(hidden, ups[slot][...], NT, preferred_element_type=F32)
            chip = meta[slot]
            values = columns(x_ref, chip, block).astype(F32) + branch - columns(t_ref, chip, block).astype(F32)
            top = (weight * values).astype(BF16)
            top_ref[at] = top
            total = total + jnp.dot(top, ups[slot][...], preferred_element_type=F32)
    sum_out[...] = total
    pre_out[...], mean_out[...] = pre_grad_of(total, slope, preact, width)


def input_grad(cot, x, down, gain, pre_grad, inverse, mean):
    grad = lax.dot_general(pre_grad, down, NT, preferred_element_type=F32)
    return (cot.astype(F32) + inverse * (grad * gain - x.astype(F32) * inverse * mean)).astype(BF16)


def leave_kernel(slots, meta, cot_ref, x_ref, gain_ref, pre_ref, inv_ref, mean_ref, *refs):
    downs, out_ref = refs[:-1], refs[-1]
    for at, slot in enumerate(slots):
        block = downs[at].shape[0]
        x, gain = columns(x_ref, meta[slot], block), columns(gain_ref, meta[slot], block)
        out_ref[at] = input_grad(cot_ref[at], x, downs[at][...], gain, pre_ref[...], inv_ref[...], mean_ref[...])


def arrive_kernel(follows, ends, width, opposite, meta, arrived_ref, top_ref, hid_ref, *refs):
    count = arrived_ref.shape[0]
    ups, refs = refs[:count], refs[count:]
    total = 0.0
    if follows:
        total = refs[0][...]
        refs = refs[1:]
    if ends:
        slope_ref, preact_ref, scaled_ref, cot_ref, pre_out, pre_t_out, mean_out, *outs = refs
        outs, parts = outs[:2], outs[2:]
    else:
        cot_ref, sum_out, *parts = refs
    for at in range(count):
        cot = jnp.where(meta.last(), top_ref[at], arrived_ref[at])
        cot_ref[at] = cot
        total = total + jnp.dot(cot, ups[at][...], preferred_element_type=F32)
        parts[at][...] = jnp.dot(hid_ref[...], cot, preferred_element_type=F32).astype(BF16)
    if not ends:
        sum_out[...] = total
        return
    pre_out[...], mean_out[...] = pre_grad_of(total, slope_ref[...], preact_ref[...], width)
    pre_t = (total * slope_ref[...]).T.astype(BF16)
    pre_t_out[...] = pre_t
    put_product(pre_t, columns(scaled_ref, meta[opposite], ups[0].shape[0]), outs)


def put_product(pre_t, scaled, halves):
    part = jnp.dot(pre_t, scaled, preferred_element_type=F32).astype(BF16)
    half = part.shape[1] // 2
    halves[0][...] = part[:, :half]
    halves[1][...] = part[:, half:]


def products_kernel(slots, meta, scaled_ref, pre_t_ref, *outs):
    for at, slot in enumerate(slots):
        halves = outs[2 * at : 2 * at + 2]
        put_product(pre_t_ref[...], columns(scaled_ref, meta[slot], 2 * halves[0].shape[1]), halves)


def stack_kernel(slots, meta, scaled_ref, pre_t_ref, out_ref):
    for at, slot in enumerate(slots):
        halves = out_ref.at[2 * at], out_ref.at[2 * at + 1]
        put_product(pre_t_ref[...], columns(scaled_ref, meta[slot], 2 * out_ref.shape[2]), halves)


def add_kernel(picks, *refs):
    out_ref = refs[-1]
    total = None
    for ref, pick in zip(refs[:-1], picks):
        value = (ref[...] if pick is None else ref[pick]).astype(F32)
        total = value if total is None else total + value
    out_ref[...] = total.astype(out_ref.dtype)


def add(out, *terms):
    arrays = [t[0] if isinstance(t, tuple) else t for t in terms]
    picks = [t[1] if isinstance(t, tuple) else None for t in terms]
    return call(functools.partial(add_kernel, picks), out, *arrays, name="add")


def split_kernel(meta, total_ref, part_ref, mine_ref, other_ref):
    half = mine_ref.shape[1]
    first = meta.first()
    low = total_ref[:, :half].astype(F32) + part_ref[:, :half].astype(F32)
    high = total_ref[:, half:].astype(F32) + part_ref[:, half:].astype(F32)
    mine_ref[...] = jnp.where(first, low, high)
    other_ref[...] = jnp.where(first, high, low).astype(BF16)


def split_halves_kernel(meta, low_ref, high_ref, low_part, high_part, mine_ref, other_ref):
    first = meta.first()
    low = low_ref[...].astype(F32) + low_part[...].astype(F32)
    high = high_ref[...].astype(F32) + high_part[...].astype(F32)
    mine_ref[...] = jnp.where(first, low, high)
    other_ref[...] = jnp.where(first, high, low).astype(BF16)


def close_kernel(tokens, mine_ref, other_ref, grad_ref):
    grad_ref[0] = ((mine_ref[...] + other_ref[...].astype(F32)) / tokens).T


def close_gain_kernel(tokens, meta, mine_ref, other_ref, down_t_ref, gain_ref, grad_ref, gain_grad_ref):
    grad = (mine_ref[...] + other_ref[...].astype(F32)) / tokens
    grad_ref[0] = grad.T
    columns_own = grad.shape[1]
    gain = columns(gain_ref, lax.axis_index("dp"), columns_own)
    gain_grad_ref[...] = jnp.sum(grad * down_t_ref[...], axis=0, keepdims=True) / gain


def finish_kernel(groups, meta, x_ref, gain_ref, pre_ref, inv_ref, mean_ref, *refs):
    slots = [slot for group in groups for slot in group]
    downs, cots = refs[: len(slots)], refs[len(slots) : len(slots) + len(groups)]
    out_ref, held, sems = refs[-3:]
    copies = []
    for group, cot_ref in zip(groups, cots):
        for at, slot in enumerate(group):
            i = len(copies)
            down = downs[i][...]
            block = down.shape[0]
            chip = meta[slot]
            x, gain = columns(x_ref, chip, block), columns(gain_ref, chip, block)
            held[i] = input_grad(cot_ref[at], x, down, gain, pre_ref[...], inv_ref[...], mean_ref[...])
            place = out_ref.at[:, pl.ds(pl.multiple_of(chip * block, block), block)]
            copies.append(pltpu.make_async_copy(held.at[i], place, sems.at[i]))
            copies[-1].start()
    for copy in copies:
        copy.wait()


def local(section_inputs, teacher_states, confidence, gains, w_down, w_up):
    sections = lax.axis_size("section")
    devices = lax.axis_size("dp")
    routes = Routes(devices)
    n, half, opposite, own, groups = routes.n, routes.half, routes.opposite, routes.own, routes.groups
    behind, ahead = routes.behind, routes.ahead
    x = section_inputs[0]
    tokens, width = x.shape
    block = width // n
    rank = w_down.shape[2]
    half_block = block // CORES
    back = [(s, s - 1) for s in range(1, sections)]

    def swap(value):
        return lax.ppermute(value, "dp", routes.partner)

    def onward(value):
        return lax.ppermute(value, "dp", routes.onward)

    rank_f32, rank_bf16 = shape(F32, tokens, rank), shape(BF16, tokens, rank)
    half_part = shape(BF16, rank, block // CORES)
    chunk, part_shape = shape(BF16, block, rank), shape(BF16, rank, block)

    def of_chip(mine, other):
        return call(
            assemble_kernel, chunk, mine, other, specs=[ANY] * 2, scratch=[pltpu.SemaphoreType.DMA((2,))], name="assemble"
        )

    def halve(value):
        return call(
            halve_kernel, shape(BF16, half_block, rank), value, specs=[ANY], scratch=[pltpu.SemaphoreType.DMA], name="halve"
        )

    down, up = w_down[0], w_up[0]
    downs, ups = {}, {}
    downs[own] = of_chip(down, swap(down))
    ups[own] = of_chip(up, swap(up))
    table = jnp.asarray(routes.table)

    def with_meta(body, outs, *args, **kw):
        specs = [SMEM] + kw.pop("specs", [VMEM] * len(args))
        return call(placed(body, sections), outs, table, *args, specs=specs, **kw)

    inverse, scaled, weight_rows, down_t = call(
        functools.partial(scale_kernel, block),
        [shape(F32, tokens, 1), shape(BF16, tokens, width), shape(F32, tokens, 1), shape(F32, rank, half_block)],
        after(x, downs[own]), gains, confidence[None], down, name="scale",
    )
    down_block, up_block = downs[own], ups[own]
    for k in range(1, half):
        earlier = []
        downs[behind(k)] = down_block = onward(after(down_block, *earlier))
        ups[behind(k)] = up_block = onward(up_block)
        downs[ahead(k)] = swap(down_block)
        ups[ahead(k)] = swap(up_block)
    earlier = [downs[ahead(half - 2)], ups[ahead(half - 2)]]
    down_far = onward(after(halve(down_block), *earlier))
    up_far = onward(halve(up_block))
    downs[opposite] = of_chip(down_far, swap(down_far))
    near = [j for j in range(n) if j != opposite]
    preact = with_meta(
        functools.partial(preact_kernel, near), rank_f32, scaled, *(downs[j] for j in near),
        flops=2 * tokens * width * rank, name="preact",
    )
    ups[opposite] = of_chip(up_far, swap(after(up_far, preact)))

    pre_grad, mean, hidden_t, slope, preact, own_sum, *tops = with_meta(
        functools.partial(top_kernel, groups, opposite),
        [rank_bf16, shape(F32, tokens, 1), shape(BF16, rank, tokens), rank_f32, rank_f32, rank_f32]
        + [shape(BF16, len(slots), tokens, block) for slots in groups],
        x, teacher_states, scaled, weight_rows, preact, downs[opposite], *(ups[j] for j in range(n)),
        flops=4 * tokens * width * rank, name="top",
    )

    def leave(slots, cot, pre_grad, mean):
        return with_meta(
            functools.partial(leave_kernel, slots), shape(BF16, len(slots), tokens, block),
            cot, x, gains, pre_grad, inverse, mean, *(downs[j] for j in slots),
            flops=2 * len(slots) * tokens * block * rank, name="leave",
        )

    def arrive(i, value, total):
        slots, kind = groups[i], shape(BF16, *value.shape)
        ends = i == len(groups) - 1
        body = functools.partial(arrive_kernel, total is not None, ends, width, opposite)
        more, outs = [] if total is None else [total], [kind, rank_f32]
        if ends:
            more += [slope, preact, scaled]
            outs = [kind, rank_bf16, shape(BF16, rank, tokens), shape(F32, tokens, 1), half_part, half_part]
        outs = with_meta(
            body, outs + [part_shape] * len(slots), value, tops[i], hidden_t, *(ups[j] for j in slots), *more,
            flops=4 * len(slots) * tokens * block * rank, name="arrive",
        )
        return outs[: -len(slots)], outs[-len(slots) :]


    def split(total, part):
        return with_meta(
            split_kernel, [shape(F32, rank, half_block), shape(BF16, rank, half_block)],
            total, part, name="split",
        )

    cots = tops
    for hop in range(sections - 1):
        sent = [leave(slots, cot, pre_grad, mean) for slots, cot in zip(groups, cots)]
        arrived = [lax.ppermute(value, "section", back) for value in sent]
        if hop < sections - 2:
            (first_cot, hidden_grad), _ = arrive(0, arrived[0], None)
            (second_cot, hidden_grad), _ = arrive(1, arrived[1], hidden_grad)
            (third_cot, pre_grad, _, mean, _, _), _ = arrive(2, arrived[2], hidden_grad)
            cots = [first_cot, second_cot, third_cot]

    def finish(some, so_far):
        slots = [j for i in some for j in groups[i]]
        args = [x, gains, pre_grad, inverse, mean, *(downs[j] for j in slots), *(cots[i] for i in some)]
        given = [] if so_far is None else [so_far]
        return with_meta(
            functools.partial(finish_kernel, [groups[i] for i in some]), shape(BF16, tokens, width), *args, *given,
            specs=[VMEM] * len(args) + [ANY] * len(given), out_specs=[ANY],
            scratch=[pltpu.VMEM((len(slots), tokens, block), BF16), pltpu.SemaphoreType.DMA((len(slots),))],
            aliases={len(args) + 1: 0} if given else {},
            flops=2 * len(slots) * tokens * block * rank, name="finish",
        )

    def step(total, part, other):
        return add(part_shape, total, part, swap(other))

    (first_cot, hidden_grad), parts = arrive(0, after(arrived[0], *sent[1:]), None)
    up_total = onward(parts[0])
    (second_cot, hidden_grad), more_parts = arrive(1, after(arrived[1], up_total), hidden_grad)
    up_sent = step(up_total, parts[1], parts[2])
    for at in range(0, len(more_parts), 2):
        up_sent = step(onward(up_sent), more_parts[at], more_parts[at + 1])
    (third_cot, pre_grad, pre_t, mean, *far), parts = arrive(2, after(arrived[2], up_sent), hidden_grad)
    cots = [first_cot, second_cot, third_cot]
    up_total = onward(step(onward(up_sent), parts[0], parts[1]))
    down_totals = [onward(value) for value in far]
    behinds = with_meta(
        functools.partial(stack_kernel, [behind(k) for k in range(1, half)]),
        shape(BF16, 2 * (half - 1), rank, half_block), scaled, pre_t, name="products",
    )
    swapped = swap(behinds)
    slots = [ahead(k) for k in range(1, half)] + [own]
    halves = with_meta(
        functools.partial(products_kernel, slots), [half_part] * (2 * len(slots)), scaled, pre_t, name="products"
    )
    input_grads = None
    for at, k in enumerate(range(half - 1, 0, -1)):
        down_totals = [
            onward(add(half_part, down_totals[c], halves[2 * (k - 1) + c], (swapped, 2 * (k - 1) + c))) for c in (0, 1)
        ]
        if at == 0:
            input_grads = finish([0, 1], None)
            down_totals[1] = after(down_totals[1], input_grads)
    input_grads = finish([2], input_grads)
    down_totals[1] = after(down_totals[1], input_grads)
    up_mine, up_other = split(up_total, parts[-1])
    up_other = swap(up_other)
    grad_up = call(
        functools.partial(close_kernel, tokens), shape(F32, 1, half_block, rank), up_mine, up_other, name="close_up"
    )
    down_mine, down_other = with_meta(
        split_halves_kernel, [shape(F32, rank, half_block), half_part], *down_totals, *halves[-2:], name="split"
    )
    down_other = swap(down_other)
    grad_down, grad_gain = with_meta(
        functools.partial(close_gain_kernel, tokens),
        [shape(F32, 1, half_block, rank), shape(F32, 1, half_block)],
        down_mine, down_other, down_t, gains, name="close_down",
    )
    return input_grads[None], grad_down, grad_up, grad_gain


def solution(mesh):
    in_specs = (
        P("section", "dp", None),
        P("dp", None),
        P("dp"),
        P("section", None),
        P("section", "dp", None),
        P("section", "dp", None),
    )
    out_specs = (
        P("section", "dp", None),
        P("section", "dp", None),
        P("section", "dp", None),
        P("section", "dp"),
    )
    return jax.shard_map(local, mesh=mesh, in_specs=in_specs, out_specs=out_specs, check_vma=False)
```

```python
import functools

import jax
import jax.numpy as jnp
import numpy as np
from jax import lax
from jax.experimental import pallas as pl
from jax.experimental.pallas import tpu as pltpu
from jax.sharding import PartitionSpec as P

Z_CHIPS = 4
CORES = 2
EPSILON = 1e-05
F32 = jnp.float32
BF16 = jnp.bfloat16
VMEM = pl.BlockSpec(memory_space=pltpu.VMEM)
SMEM = pl.BlockSpec(memory_space=pltpu.SMEM)
ANY = pl.BlockSpec(memory_space=pl.ANY)
NT = (((1,), (1,)), ((), ()))


def ring_of_chips(chips):
    rows = chips // Z_CHIPS
    cycle = []
    for z in range(Z_CHIPS):
        ys = range(1, rows) if z % 2 == 0 else range(rows - 1, 0, -1)
        cycle += [z * rows + y for y in ys]
    return cycle + [z * rows for z in range(Z_CHIPS - 1, -1, -1)]


class Routes:
    def __init__(self, devices):
        ring = ring_of_chips(devices // CORES)
        n = self.n = len(ring)
        half = self.half = n // 2
        self.partner = [(i, i ^ 1) for i in range(devices)]
        self.onward = [
            (ring[i] * CORES + c, ring[(i + 1 - 2 * c) % n] * CORES + c) for c in range(CORES) for i in range(n)
        ]
        steps = [s for k in range(1, half) for s in (-k, k)] + [half, 0]
        self.table = np.zeros((devices, n), np.int32)
        for i, chip in enumerate(ring):
            for c in range(CORES):
                self.table[chip * CORES + c] = [ring[(i + (1 - 2 * c) * s) % n] for s in steps]
        self.opposite, self.own = n - 2, n - 1
        leaving = [self.opposite] + [f(k) for k in range(half - 1, 0, -1) for f in (self.ahead, self.behind)] + [self.own]
        self.groups = [leaving[:3], leaving[3:-3], leaving[-3:]]

    def behind(self, k):
        return 2 * k - 2

    def ahead(self, k):
        return 2 * k - 1


def after(value, *earlier):
    return lax.optimization_barrier((value, *earlier))[0] if earlier else value


def call(body, outs, *args, specs=None, out_specs=None, scratch=(), flops=0, aliases=None, vmem=8, name=None):
    single = not isinstance(outs, (list, tuple))
    outs = [outs] if single else list(outs)
    moved = sum(a.size * a.dtype.itemsize for a in args) + sum(o.size * o.dtype.itemsize for o in outs)
    result = pl.pallas_call(
        body,
        in_specs=specs or [VMEM] * len(args),
        out_specs=out_specs or [VMEM] * len(outs),
        out_shape=outs,
        scratch_shapes=scratch,
        input_output_aliases=aliases or {},
        cost_estimate=pl.CostEstimate(flops=flops, bytes_accessed=moved // 4, transcendentals=0),
        compiler_params=pltpu.CompilerParams(vmem_limit_bytes=vmem << 20),
        name=name,
    )(*args)
    return result[0] if single else result


class Place:
    def __init__(self, sections, table_ref):
        self.table, self.sections, self.n = table_ref, sections, table_ref.shape[1]

    def __getitem__(self, slot):
        return self.table[lax.axis_index("dp"), slot]

    def first(self):
        return lax.axis_index("dp") % CORES == 0

    def last(self):
        return lax.axis_index("section") == self.sections - 1


def placed(body, sections):
    def kernel(table_ref, *refs):
        body(Place(sections, table_ref), *refs)

    return kernel


def shape(dtype, *dims):
    return jax.ShapeDtypeStruct(dims, dtype)


def columns(ref, chip, block):
    return ref[:, pl.ds(pl.multiple_of(chip * block, block), block)]


def scale_kernel(block, x_ref, gain_ref, conf_ref, down_ref, inv_ref, scaled_ref, weight_ref, down_t_ref):
    tokens, width = x_ref.shape
    squares = jnp.zeros((tokens, block), F32)
    for at in range(0, width, block):
        values = x_ref[:, at : at + block].astype(F32)
        squares = squares + values * values
    inverse = lax.rsqrt(jnp.sum(squares, axis=-1, keepdims=True) / width + EPSILON)
    inv_ref[...] = inverse
    for at in range(0, width, block):
        values = x_ref[:, at : at + block].astype(F32)
        scaled_ref[:, at : at + block] = ((values * inverse) * gain_ref[:, at : at + block]).astype(BF16)
    weights = jnp.broadcast_to(conf_ref[...].astype(F32) / 256.0, (tokens, tokens))
    row = lax.broadcasted_iota(jnp.int32, (tokens, tokens), 0)
    column = lax.broadcasted_iota(jnp.int32, (tokens, tokens), 1)
    weight_ref[...] = jnp.sum(jnp.where(row == column, weights, 0.0), axis=1, keepdims=True)
    down_t_ref[...] = down_ref[...].astype(F32).T


def assemble_kernel(mine_ref, other_ref, out_ref, sems):
    rows = mine_ref.shape[0]
    core = lax.axis_index("dp") % CORES
    copies = []
    for i, (ref, place) in enumerate(((mine_ref, core), (other_ref, 1 - core))):
        out = out_ref.at[pl.ds(pl.multiple_of(place * rows, rows), rows)]
        copies.append(pltpu.make_async_copy(ref, out, sems.at[i]))
        copies[-1].start()
    for copy in copies:
        copy.wait()


def halve_kernel(block_ref, out_ref, sem):
    rows = out_ref.shape[0]
    core = lax.axis_index("dp") % CORES
    copy = pltpu.make_async_copy(block_ref.at[pl.ds(pl.multiple_of(core * rows, rows), rows)], out_ref, sem)
    copy.start()
    copy.wait()


def pre_grad_of(hidden_grad, slope, preact, width):
    pre_grad = (hidden_grad * slope).astype(BF16)
    return pre_grad, jnp.sum(pre_grad.astype(F32) * preact, axis=-1, keepdims=True) / width


def preact_kernel(slots, meta, scaled_ref, *refs):
    downs, out_ref = refs[:-1], refs[-1]
    total = 0.0
    for slot, down_ref in zip(slots, downs):
        scaled = columns(scaled_ref, meta[slot], down_ref.shape[0])
        total = total + jnp.dot(scaled, down_ref[...], preferred_element_type=F32)
    out_ref[...] = total


def top_kernel(groups, opposite, meta, x_ref, t_ref, scaled_ref, weight_ref, sum_ref, down_ref, *refs):
    n = meta.n
    ups, (pre_out, mean_out, hid_out, slope_out, preact_out, sum_out, *tops) = refs[:n], refs[n:]
    width = x_ref.shape[1]
    block = width // n
    far = columns(scaled_ref, meta[opposite], block)
    preact = sum_ref[...] + jnp.dot(far, down_ref[...], preferred_element_type=F32)
    sigmoid_val = 1.0 / (1.0 + jnp.exp(-preact))
    slope = sigmoid_val * (1.0 + preact * (1.0 - sigmoid_val))
    hidden = preact * sigmoid_val
    preact_out[...] = preact
    slope_out[...] = slope
    hid_out[...] = hidden.T.astype(BF16)
    hidden = hidden.astype(BF16)
    weight = weight_ref[...]
    total = jnp.zeros_like(preact)
    for group, top_ref in zip(groups, tops):
        for at, slot in enumerate(group):
            branch = lax.dot_general(hidden, ups[slot][...], NT, preferred_element_type=F32)
            chip = meta[slot]
            values = columns(x_ref, chip, block).astype(F32) + branch - columns(t_ref, chip, block).astype(F32)
            top = (weight * values).astype(BF16)
            top_ref[at] = top
            total = total + jnp.dot(top, ups[slot][...], preferred_element_type=F32)
    sum_out[...] = total
    pre_out[...], mean_out[...] = pre_grad_of(total, slope, preact, width)


def input_grad(cot, x, down, gain, pre_grad, inverse, mean):
    grad = lax.dot_general(pre_grad, down, NT, preferred_element_type=F32)
    return (cot.astype(F32) + inverse * (grad * gain - x.astype(F32) * inverse * mean)).astype(BF16)


def leave_kernel(slots, meta, cot_ref, x_ref, gain_ref, pre_ref, inv_ref, mean_ref, *refs):
    downs, out_ref = refs[:-1], refs[-1]
    for at, slot in enumerate(slots):
        block = downs[at].shape[0]
        x, gain = columns(x_ref, meta[slot], block), columns(gain_ref, meta[slot], block)
        out_ref[at] = input_grad(cot_ref[at], x, downs[at][...], gain, pre_ref[...], inv_ref[...], mean_ref[...])


def arrive_kernel(follows, ends, width, opposite, meta, arrived_ref, top_ref, hid_ref, *refs):
    count = arrived_ref.shape[0]
    ups, refs = refs[:count], refs[count:]
    total = 0.0
    if follows:
        total = refs[0][...]
        refs = refs[1:]
    if ends:
        slope_ref, preact_ref, scaled_ref, cot_ref, pre_out, pre_t_out, mean_out, *outs = refs
        far_out, *parts = outs
    else:
        cot_ref, sum_out, *parts = refs
    for at in range(count):
        cot = jnp.where(meta.last(), top_ref[at], arrived_ref[at])
        cot_ref[at] = cot
        total = total + jnp.dot(cot, ups[at][...], preferred_element_type=F32)
        parts[at][...] = jnp.dot(hid_ref[...], cot, preferred_element_type=F32).astype(BF16)
    if not ends:
        sum_out[...] = total
        return
    pre_out[...], mean_out[...] = pre_grad_of(total, slope_ref[...], preact_ref[...], width)
    pre_t = (total * slope_ref[...]).T.astype(BF16)
    pre_t_out[...] = pre_t
    far = jnp.dot(pre_t, columns(scaled_ref, meta[opposite], ups[0].shape[0]), preferred_element_type=F32)
    far_out[...] = far.astype(BF16)


def put_product(pre_t, scaled, halves):
    part = jnp.dot(pre_t, scaled, preferred_element_type=F32).astype(BF16)
    half = part.shape[1] // 2
    halves[0][...] = part[:, :half]
    halves[1][...] = part[:, half:]


def products_kernel(slots, meta, scaled_ref, pre_t_ref, *outs):
    for at, slot in enumerate(slots):
        halves = outs[2 * at : 2 * at + 2]
        put_product(pre_t_ref[...], columns(scaled_ref, meta[slot], 2 * halves[0].shape[1]), halves)


def stack_kernel(slots, meta, scaled_ref, pre_t_ref, out_ref):
    for at, slot in enumerate(slots):
        halves = out_ref.at[2 * at], out_ref.at[2 * at + 1]
        put_product(pre_t_ref[...], columns(scaled_ref, meta[slot], 2 * out_ref.shape[2]), halves)


def add_kernel(picks, *refs):
    out_ref = refs[-1]
    total = None
    for ref, pick in zip(refs[:-1], picks):
        value = (ref[...] if pick is None else ref[pick]).astype(F32)
        total = value if total is None else total + value
    out_ref[...] = total.astype(out_ref.dtype)


def add(out, *terms):
    arrays = [t[0] if isinstance(t, tuple) else t for t in terms]
    picks = [t[1] if isinstance(t, tuple) else None for t in terms]
    return call(functools.partial(add_kernel, picks), out, *arrays, name="add")


def split_kernel(meta, total_ref, part_ref, mine_ref, other_ref):
    half = mine_ref.shape[1]
    first = meta.first()
    low = total_ref[:, :half].astype(F32) + part_ref[:, :half].astype(F32)
    high = total_ref[:, half:].astype(F32) + part_ref[:, half:].astype(F32)
    mine_ref[...] = jnp.where(first, low, high)
    other_ref[...] = jnp.where(first, high, low).astype(BF16)


def split_halves_kernel(meta, low_ref, high_ref, low_part, high_part, mine_ref, other_ref):
    first = meta.first()
    low = low_ref[...].astype(F32) + low_part[...].astype(F32)
    high = high_ref[...].astype(F32) + high_part[...].astype(F32)
    mine_ref[...] = jnp.where(first, low, high)
    other_ref[...] = jnp.where(first, high, low).astype(BF16)


def close_kernel(tokens, mine_ref, other_ref, grad_ref):
    grad_ref[0] = ((mine_ref[...] + other_ref[...].astype(F32)) / tokens).T


def close_gain_kernel(tokens, meta, mine_ref, other_ref, down_t_ref, gain_ref, grad_ref, gain_grad_ref):
    grad = (mine_ref[...] + other_ref[...].astype(F32)) / tokens
    grad_ref[0] = grad.T
    columns_own = grad.shape[1]
    gain = columns(gain_ref, lax.axis_index("dp"), columns_own)
    gain_grad_ref[...] = jnp.sum(grad * down_t_ref[...], axis=0, keepdims=True) / gain


def finish_kernel(groups, meta, x_ref, gain_ref, pre_ref, inv_ref, mean_ref, *refs):
    slots = [slot for group in groups for slot in group]
    downs, cots = refs[: len(slots)], refs[len(slots) : len(slots) + len(groups)]
    out_ref, held, sems = refs[-3:]
    copies = []
    for group, cot_ref in zip(groups, cots):
        for at, slot in enumerate(group):
            i = len(copies)
            down = downs[i][...]
            block = down.shape[0]
            chip = meta[slot]
            x, gain = columns(x_ref, chip, block), columns(gain_ref, chip, block)
            held[i] = input_grad(cot_ref[at], x, down, gain, pre_ref[...], inv_ref[...], mean_ref[...])
            place = out_ref.at[:, pl.ds(pl.multiple_of(chip * block, block), block)]
            copies.append(pltpu.make_async_copy(held.at[i], place, sems.at[i]))
            copies[-1].start()
    for copy in copies:
        copy.wait()


def local(section_inputs, teacher_states, confidence, gains, w_down, w_up):
    sections = lax.axis_size("section")
    devices = lax.axis_size("dp")
    routes = Routes(devices)
    n, half, opposite, own, groups = routes.n, routes.half, routes.opposite, routes.own, routes.groups
    behind, ahead = routes.behind, routes.ahead
    x = section_inputs[0]
    tokens, width = x.shape
    block = width // n
    rank = w_down.shape[2]
    half_block = block // CORES
    back = [(s, s - 1) for s in range(1, sections)]

    def swap(value):
        return lax.ppermute(value, "dp", routes.partner)

    def onward(value):
        return lax.ppermute(value, "dp", routes.onward)

    rank_f32, rank_bf16 = shape(F32, tokens, rank), shape(BF16, tokens, rank)
    half_part = shape(BF16, rank, block // CORES)
    chunk, part_shape = shape(BF16, block, rank), shape(BF16, rank, block)

    def of_chip(mine, other):
        return call(
            assemble_kernel, chunk, mine, other, specs=[ANY] * 2, scratch=[pltpu.SemaphoreType.DMA((2,))], name="assemble"
        )

    def halve(value):
        return call(
            halve_kernel, shape(BF16, half_block, rank), value, specs=[ANY], scratch=[pltpu.SemaphoreType.DMA], name="halve"
        )

    down, up = w_down[0], w_up[0]
    downs, ups = {}, {}
    downs[own] = of_chip(down, swap(down))
    ups[own] = of_chip(up, swap(up))
    table = jnp.asarray(routes.table)

    def with_meta(body, outs, *args, **kw):
        specs = [SMEM] + kw.pop("specs", [VMEM] * len(args))
        return call(placed(body, sections), outs, table, *args, specs=specs, **kw)

    inverse, scaled, weight_rows, down_t = call(
        functools.partial(scale_kernel, block),
        [shape(F32, tokens, 1), shape(BF16, tokens, width), shape(F32, tokens, 1), shape(F32, rank, half_block)],
        after(x, downs[own]), gains, confidence[None], down, name="scale",
    )
    down_block, up_block = downs[own], ups[own]
    for k in range(1, half):
        earlier = []
        downs[behind(k)] = down_block = onward(after(down_block, *earlier))
        ups[behind(k)] = up_block = onward(up_block)
        downs[ahead(k)] = swap(down_block)
        ups[ahead(k)] = swap(up_block)
    earlier = [downs[ahead(half - 2)], ups[ahead(half - 2)]]
    down_far = onward(after(halve(down_block), *earlier))
    up_far = onward(halve(up_block))
    downs[opposite] = of_chip(down_far, swap(down_far))
    near = [j for j in range(n) if j != opposite]
    preact = with_meta(
        functools.partial(preact_kernel, near), rank_f32, scaled, *(downs[j] for j in near),
        flops=2 * tokens * width * rank, name="preact",
    )
    ups[opposite] = of_chip(up_far, swap(after(up_far, preact)))

    pre_grad, mean, hidden_t, slope, preact, own_sum, *tops = with_meta(
        functools.partial(top_kernel, groups, opposite),
        [rank_bf16, shape(F32, tokens, 1), shape(BF16, rank, tokens), rank_f32, rank_f32, rank_f32]
        + [shape(BF16, len(slots), tokens, block) for slots in groups],
        x, teacher_states, scaled, weight_rows, preact, downs[opposite], *(ups[j] for j in range(n)),
        flops=4 * tokens * width * rank, name="top",
    )

    def leave(slots, cot, pre_grad, mean):
        return with_meta(
            functools.partial(leave_kernel, slots), shape(BF16, len(slots), tokens, block),
            cot, x, gains, pre_grad, inverse, mean, *(downs[j] for j in slots),
            flops=2 * len(slots) * tokens * block * rank, name="leave",
        )

    def arrive(i, value, total):
        slots, kind = groups[i], shape(BF16, *value.shape)
        ends = i == len(groups) - 1
        body = functools.partial(arrive_kernel, total is not None, ends, width, opposite)
        more, outs = [] if total is None else [total], [kind, rank_f32]
        if ends:
            more += [slope, preact, scaled]
            outs = [kind, rank_bf16, shape(BF16, rank, tokens), shape(F32, tokens, 1), part_shape]
        outs = with_meta(
            body, outs + [part_shape] * len(slots), value, tops[i], hidden_t, *(ups[j] for j in slots), *more,
            flops=4 * len(slots) * tokens * block * rank, name="arrive",
        )
        return outs[: -len(slots)], outs[-len(slots) :]


    def split(total, part):
        return with_meta(
            split_kernel, [shape(F32, rank, half_block), shape(BF16, rank, half_block)],
            total, part, name="split",
        )

    cots = tops
    for hop in range(sections - 1):
        sent = [leave(slots, cot, pre_grad, mean) for slots, cot in zip(groups, cots)]
        arrived = [lax.ppermute(value, "section", back) for value in sent]
        if hop < sections - 2:
            (first_cot, hidden_grad), _ = arrive(0, arrived[0], None)
            (second_cot, hidden_grad), _ = arrive(1, arrived[1], hidden_grad)
            (third_cot, pre_grad, _, mean, _), _ = arrive(2, arrived[2], hidden_grad)
            cots = [first_cot, second_cot, third_cot]

    def finish(some, so_far):
        slots = [j for i in some for j in groups[i]]
        args = [x, gains, pre_grad, inverse, mean, *(downs[j] for j in slots), *(cots[i] for i in some)]
        given = [] if so_far is None else [so_far]
        return with_meta(
            functools.partial(finish_kernel, [groups[i] for i in some]), shape(BF16, tokens, width), *args, *given,
            specs=[VMEM] * len(args) + [ANY] * len(given), out_specs=[ANY],
            scratch=[pltpu.VMEM((len(slots), tokens, block), BF16), pltpu.SemaphoreType.DMA((len(slots),))],
            aliases={len(args) + 1: 0} if given else {},
            flops=2 * len(slots) * tokens * block * rank, name="finish",
        )

    def step(total, part, other):
        return add(part_shape, total, part, swap(other))

    (first_cot, hidden_grad), parts = arrive(0, after(arrived[0], *sent[1:]), None)
    up_total = onward(parts[0])
    (second_cot, hidden_grad), more_parts = arrive(1, after(arrived[1], up_total), hidden_grad)
    up_sent = step(up_total, parts[1], parts[2])
    for at in range(0, len(more_parts), 2):
        up_sent = step(onward(up_sent), more_parts[at], more_parts[at + 1])
    (third_cot, pre_grad, pre_t, mean, far), parts = arrive(2, after(arrived[2], up_sent), hidden_grad)
    cots = [first_cot, second_cot, third_cot]
    up_total = onward(step(onward(up_sent), parts[0], parts[1]))
    far = onward(far)
    down_totals = [(far, (slice(None), slice(c * half_block, (c + 1) * half_block))) for c in (0, 1)]
    behinds = with_meta(
        functools.partial(stack_kernel, [behind(k) for k in range(1, half)]),
        shape(BF16, 2 * (half - 1), rank, half_block), scaled, pre_t, name="products",
    )
    swapped = swap(behinds)
    slots = [ahead(k) for k in range(1, half)] + [own]
    halves = with_meta(
        functools.partial(products_kernel, slots), [half_part] * (2 * len(slots)), scaled, pre_t, name="products"
    )
    input_grads = None
    for at, k in enumerate(range(half - 1, 0, -1)):
        down_totals = [
            onward(add(half_part, down_totals[c], halves[2 * (k - 1) + c], (swapped, 2 * (k - 1) + c))) for c in (0, 1)
        ]
        if at == 0:
            input_grads = finish([0, 1], None)
            down_totals[1] = after(down_totals[1], input_grads)
    input_grads = finish([2], input_grads)
    down_totals[1] = after(down_totals[1], input_grads)
    up_mine, up_other = split(up_total, parts[-1])
    up_other = swap(up_other)
    grad_up = call(
        functools.partial(close_kernel, tokens), shape(F32, 1, half_block, rank), up_mine, up_other, name="close_up"
    )
    down_mine, down_other = with_meta(
        split_halves_kernel, [shape(F32, rank, half_block), half_part], *down_totals, *halves[-2:], name="split"
    )
    down_other = swap(down_other)
    grad_down, grad_gain = with_meta(
        functools.partial(close_gain_kernel, tokens),
        [shape(F32, 1, half_block, rank), shape(F32, 1, half_block)],
        down_mine, down_other, down_t, gains, name="close_down",
    )
    return input_grads[None], grad_down, grad_up, grad_gain


def solution(mesh):
    in_specs = (
        P("section", "dp", None),
        P("dp", None),
        P("dp"),
        P("section", None),
        P("section", "dp", None),
        P("section", "dp", None),
    )
    out_specs = (
        P("section", "dp", None),
        P("section", "dp", None),
        P("section", "dp", None),
        P("section", "dp"),
    )
    return jax.shard_map(local, mesh=mesh, in_specs=in_specs, out_specs=out_specs, check_vma=False)
```
